32 devices in a mesh: unit: 2 (over y), row: 16 (over z, x, core).
Axes of the slice: x: 2, y: 2, z: 4, core: 2. Of those that a mesh axis runs over, the one named last changes fastest.
Arguments:
- tokens: bfloat16 [16384, 768], P('row'), may hold values from -5 to 5
- doc_ids: int32 [1, 16384], replicated, may hold values from 0 to 11, never falling along the last dimension, each value on 1 to 4096 neighbouring positions
- valid: int32 [1, 16384], replicated, may hold values from 0 to 1, as said below
- ln1_gain: float32 [768], replicated, may hold values from 0.5 to 1.5
- ln1_shift: float32 [768], replicated, may hold values from -0.3 to 0.3
- w_query: bfloat16 [768, 768], P(None, 'unit'), may hold values from -0.21875 to 0.21875
- b_query: float32 [768], P('unit'), may hold values from -3 to 3
- w_key: bfloat16 [768, 768], P(None, 'unit'), may hold values from -0.21875 to 0.21875
- w_value: bfloat16 [768, 768], P(None, 'unit'), may hold values from -0.21875 to 0.21875
- b_value: float32 [768], P('unit'), may hold values from -0.3 to 0.3
- w_out: bfloat16 [768, 768], P('unit'), may hold values from -1.75 to 1.75
- b_out: float32 [768], replicated, may hold values from -1.2 to 1.2
- ln2_gain: float32 [768], replicated, may hold values from 0.5 to 1.5
- ln2_shift: float32 [768], replicated, may hold values from -0.6 to 0.6
- w_up: bfloat16 [768, 3072], P(None, 'unit'), may hold values from -0.21875 to 0.21875
- b_up: float32 [3072], P('unit'), may hold values from -3 to 3
- w_down: bfloat16 [3072, 768], P('unit'), may hold values from -0.109375 to 0.109375
- b_down: float32 [768], replicated, may hold values from -1.2 to 1.2
- cotangent: bfloat16 [16384, 768], P('row'), may hold values from -5 to 5
Outputs:
- mixed_out: bfloat16 [16384, 768], P('row')
- grad_tokens: float32 [16384, 768], P('row')
- grad_ln1_gain: float32 [768], replicated
- grad_ln1_shift: float32 [768], replicated
- grad_w_query: float32 [768, 768], P(None, 'unit')
- grad_b_query: float32 [768], P('unit')
- grad_w_key: float32 [768, 768], P(None, 'unit')
- grad_w_value: float32 [768, 768], P(None, 'unit')
- grad_b_value: float32 [768], P('unit')
- grad_w_out: float32 [768, 768], P('unit')
- grad_b_out: float32 [768], replicated
- grad_ln2_gain: float32 [768], replicated
- grad_ln2_shift: float32 [768], replicated
- grad_w_up: float32 [768, 3072], P(None, 'unit')
- grad_b_up: float32 [3072], P('unit')
- grad_w_down: float32 [3072, 768], P('unit')
- grad_b_down: float32 [768], replicated
The draws below stay inside these ranges and needn't reach their ends.
Inputs may be any that keep to these rules, and one draw needn't show every extreme that they name: `valid`: every sequence but the last is all ones; the last ends in a run of 2048 to 8192 zeros.
All inputs are finite; a program needn't handle non-finite values.
Results may differ from the reference program's by a relative error of at most 0.012.
The reference program's roundings to bfloat16 on the way count: a program that leaves them out, or rounds other values in their place, can miss the bound.
Values may be sent and summed in bfloat16 or wider, within the bound.
No kernel may reach another device: no remote copies, remote signals or barrier semaphores. Data moves between devices by JAX's collectives and lax.ppermute only.
A program may use at most 256 MiB of HBM per device.

```python
import math
from functools import reduce
import jax
import jax.numpy as jnp
import numpy as np
from jax import lax

D = 768
HEADS = 16
HEAD_DIM = 48
FF = 3072
SEG0 = 1024
BRANCHES = 5
SEQS = 1
DOCS = 12
SEQ = 16384
DOC_MOST = 4096
TOKENS = 16384


def draw_valid(key, part):
    padded = jax.random.randint(key, (), SEQ // 8, SEQ // 2 + 1)
    position = jnp.arange(SEQS * SEQ, dtype=jnp.int32).reshape(SEQS, SEQ)
    return jnp.where(position < SEQS * SEQ - padded, 1, 0).astype(jnp.int32)


def shard_levels(stream_key, dims, cuts, least, high):
    factor_of = 1.0
    for axis_at, shards_of in cuts:
        heights = jax.random.uniform(jax.random.fold_in(jax.random.fold_in(stream_key, 6), axis_at), (shards_of,), jnp.float32, least / len(cuts), high / len(cuts))
        factor_of = factor_of * jnp.repeat(jnp.exp(heights), dims[axis_at] // shards_of).reshape((-1,) + (1,) * (len(dims) - 1 - axis_at))
    return factor_of


def split_up(number_of, total, reach, slope):
    portions = [(1 << 20) // math.isqrt(rank ** slope) + 1 for rank in range(2, number_of + 1)]
    surplus, holding = total - reach - (number_of - 1), [1] * (number_of - 1)
    while surplus > 0:
        candidates = [i for i in range(number_of - 1) if holding[i] < reach]
        whole, remaining = sum([portions[i] for i in candidates]), surplus
        for i in candidates:
            addition = min(reach - holding[i], max(1, remaining * portions[i] // whole), surplus)
            holding[i] = holding[i] + addition
            surplus = surplus - addition
    return np.array([reach] + holding)


def ragged(own_key, amount, total, limit, slope):
    if amount == 2:
        one = jax.random.randint(own_key, (), max(1, total - limit), min(limit, total - 1) + 1)
        return jnp.stack([one, total - one])
    sizes = jnp.asarray(split_up(amount, total, limit, slope), jnp.int32)
    couples = (amount - 1) // 2
    source_of, taker = sizes[1:1 + 2 * couples:2], sizes[2:2 + 2 * couples:2]
    margin = jnp.minimum(source_of - 1, limit - taker)
    shifted = jax.random.randint(jax.random.fold_in(own_key, 1), (couples,), 0, 1 << 20) % (margin + 1)
    sizes = sizes.at[1:1 + 2 * couples:2].set(source_of - shifted).at[2:2 + 2 * couples:2].set(taker + shifted)
    return sizes[jax.random.permutation(jax.random.fold_in(own_key, 2), amount)]


def bell_draw(stream_key, shape, deviation, limit, cuts=(), held_as=jnp.bfloat16):
    entries = deviation * jax.random.normal(stream_key, shape, jnp.float32)
    if cuts:
        entries = entries * shard_levels(stream_key, shape, cuts, -0.22, 0.18)
    return jnp.clip(entries, -limit, limit).astype(held_as)


def setup_inputs(seed: int = 0) -> dict:
    keys = jax.random.split(jax.random.key(seed), 20)
    return {
        "tokens": bell_draw(keys[0], (TOKENS, D), 1.0, 5.0, ((0, 16),)),
        "doc_ids": jax.vmap(lambda own: jnp.searchsorted(jnp.cumsum(ragged(own, DOCS, SEQ, DOC_MOST, 2)), jnp.arange(SEQ), side="right"))(jax.random.split(keys[1], SEQS)).reshape((SEQS, SEQ)).astype(jnp.int32),
        "valid": draw_valid(jax.random.fold_in(keys[19], 71), 0),
        "ln1_gain": jnp.clip(1.0 + 0.1 * jax.random.normal(keys[3], (D,), jnp.float32), 0.5, 1.5),
        "ln1_shift": bell_draw(keys[4], (D,), 0.05, 0.3, (), jnp.float32),
        "w_query": bell_draw(keys[5], (D, D), D ** -0.5, 0.21875, ((1, 2),)),
        "b_query": bell_draw(keys[6], (D,), 0.5, 3.0, ((0, 2),), jnp.float32),
        "w_key": bell_draw(keys[7], (D, D), D ** -0.5, 0.21875, ((1, 2),)),
        "w_value": bell_draw(keys[8], (D, D), D ** -0.5, 0.21875, ((1, 2),)),
        "b_value": bell_draw(keys[9], (D,), 0.05, 0.3, ((0, 2),), jnp.float32),
        "w_out": bell_draw(keys[10], (D, D), (max(D // 64, 4)) ** -0.5, 1.75, ((0, 2),)),
        "b_out": bell_draw(keys[11], (D,), 0.2, 1.2, (), jnp.float32),
        "ln2_gain": jnp.clip(1.0 + 0.1 * jax.random.normal(keys[12], (D,), jnp.float32), 0.5, 1.5),
        "ln2_shift": bell_draw(keys[13], (D,), 0.1, 0.6, (), jnp.float32),
        "w_up": bell_draw(keys[14], (D, FF), D ** -0.5, 0.21875, ((1, 2),)),
        "b_up": bell_draw(keys[15], (FF,), 0.5, 3.0, ((0, 2),), jnp.float32),
        "w_down": bell_draw(keys[16], (FF, D), FF ** -0.5, 0.109375, ((0, 2),)),
        "b_down": bell_draw(keys[17], (D,), 0.2, 1.2, (), jnp.float32),
        "cotangent": bell_draw(keys[18], (TOKENS, D), 1.0, 5.0, ((0, 16),)),
    }


EPSILON = 1e-05
MASKED = -1000000000.0
GELU_SCALE = 0.7978845608028654
HIGHEST = lax.Precision.HIGHEST

@jax.custom_vjp
def low(v):
    return lax.optimization_barrier(v.astype(jnp.bfloat16)).astype(jnp.float32)

@jax.custom_vjp
def low_back(v):
    return v

def low_keep(v):
    return (low(v), None)

def low_pass(kept, grad):
    return (grad,)

def back_keep(v):
    return (v, None)

def back_low(kept, grad):
    return (low(grad),)
low.defvjp(low_keep, low_pass)
low_back.defvjp(back_keep, back_low)

def layer_norm(values, norm_gain, norm_shift):
    row_mean = lax.optimization_barrier(jnp.mean(values, axis=-1, keepdims=True))
    centred = values - row_mean
    row_var = lax.optimization_barrier(jnp.mean(centred * centred, axis=-1, keepdims=True))
    return centred * lax.rsqrt(row_var + EPSILON) * norm_gain + norm_shift

def gelu_tanh(values):
    cubic = values + 0.044715 * values * values * values
    return 0.5 * values * (1.0 + jnp.tanh(GELU_SCALE * cubic))

def matmul(left_side, right_side):
    return jnp.dot(left_side, right_side, preferred_element_type=jnp.float32, precision=HIGHEST)

def attend(parts):
    queries, key_units, value_units, query_tags, key_tags = parts
    scores = low_back(jnp.einsum('hqd,hkd->hqk', queries, key_units, precision=HIGHEST))
    scores = jnp.where(query_tags[:, :, None] == key_tags[:, None, :], scores, MASKED)
    row_peak = lax.optimization_barrier(jnp.max(scores, axis=-1, keepdims=True))
    weights = jnp.exp(scores - row_peak)
    weight_sum = lax.optimization_barrier(jnp.sum(weights, axis=-1, keepdims=True))
    attn_probs = low(weights / weight_sum)
    outputs = low_back(jnp.einsum('hqk,hkd->hqd', attn_probs, value_units, precision=HIGHEST))
    return (outputs, row_peak[..., 0] + jnp.log(weight_sum[..., 0]))

def dilated_attention(query_rows, key_rows, value_rows, slot_tags):
    length = query_rows.shape[0]
    head_list = np.arange(HEADS)
    branch_outs = []
    branch_lses = []
    chosen = []
    for branch in range(BRANCHES):
        stride = 2 ** branch
        segments = length // (SEG0 * stride)
        offsets = head_list % stride

        def select(source):
            shaped = source.reshape((segments, SEG0, stride) + source.shape[1:])
            return shaped[:, :, offsets, head_list]
        tag_rows = select(jnp.broadcast_to(slot_tags[:, None], (length, HEADS)))
        tag_rows = jnp.transpose(tag_rows, (0, 2, 1))
        parts = (jnp.transpose(select(query_rows), (0, 2, 1, 3)), jnp.transpose(select(key_rows), (0, 2, 1, 3)), jnp.transpose(select(value_rows), (0, 2, 1, 3)), tag_rows, tag_rows)
        outputs, log_total = lax.map(jax.checkpoint(attend), parts)
        hit_mask = np.arange(stride)[:, None] == offsets[None, :]
        spread_out = jnp.where(hit_mask[None, None, :, :, None], jnp.transpose(outputs, (0, 2, 1, 3))[:, :, None], 0.0)
        spread_lse = jnp.where(hit_mask[None, None], jnp.transpose(log_total, (0, 2, 1))[:, :, None], 0.0)
        branch_outs.append(spread_out.reshape(length, HEADS, HEAD_DIM))
        branch_lses.append(spread_lse.reshape(length, HEADS))
        chosen.append(np.arange(length)[:, None] % stride == offsets[None, :])
    peak_lse = reduce(jnp.maximum, [jnp.where(mask_here, lse_here, MASKED) for mask_here, lse_here in zip(chosen, branch_lses)])
    weights = [jnp.where(mask_here, jnp.exp(jnp.where(mask_here, lse_here, peak_lse) - peak_lse), 0.0) for mask_here, lse_here in zip(chosen, branch_lses)]
    weight_sum = reduce(jnp.add, weights)
    merged = reduce(jnp.add, [(weight_here / weight_sum)[:, :, None] * out_here for weight_here, out_here in zip(weights, branch_outs)])
    return merged.reshape(length, HEADS * HEAD_DIM)

def forward(params, residual, slot_tags):
    ln1_gain, ln1_shift, w_query, b_query, w_key, w_value, b_value, w_out, b_out, ln2_gain, ln2_shift, w_up, b_up, w_down, b_down = params
    scaling = HEAD_DIM ** (-0.5)
    head_shape = (residual.shape[0], HEADS, HEAD_DIM)
    normed = low(layer_norm(residual, ln1_gain, ln1_shift))
    query_rows = low(low_back((matmul(normed, w_query) + b_query) * scaling)).reshape(head_shape)
    key_rows = low(low_back(matmul(normed, w_key))).reshape(head_shape)
    value_rows = low(low_back(matmul(normed, w_value) + b_value)).reshape(head_shape)
    merged = low(dilated_attention(query_rows, key_rows, value_rows, slot_tags))
    middle = residual + low_back(matmul(merged, w_out) + b_out)
    normed2 = low(layer_norm(middle, ln2_gain, ln2_shift))
    hidden = low(gelu_tanh(low_back(matmul(normed2, w_up) + b_up)))
    return middle + low_back(matmul(hidden, w_down) + b_down)

def reference(tokens, doc_ids, valid, ln1_gain, ln1_shift, w_query, b_query, w_key, w_value, b_value, w_out, b_out, ln2_gain, ln2_shift, w_up, b_up, w_down, b_down, cotangent):
    params = tuple((item.astype(jnp.float32) for item in (ln1_gain, ln1_shift, w_query, b_query, w_key, w_value, b_value, w_out, b_out, ln2_gain, ln2_shift, w_up, b_up, w_down, b_down)))
    slot_tags = jnp.where(valid == 1, doc_ids, -1).astype(jnp.int32)
    inputs = tokens.astype(jnp.float32).reshape(SEQS, SEQ, D)
    backs = cotangent.astype(jnp.float32).reshape(SEQS, SEQ, D)

    def one_sequence(running, item):
        values, marks, back_rows = item
        result, pullback = jax.vjp(lambda weights, rows_in: forward(weights, rows_in, marks), params, values)
        param_grads, input_grads = pullback(back_rows)
        return (jax.tree.map(jnp.add, running, param_grads), (result, input_grads))
    zeros_start = jax.tree.map(jnp.zeros_like, params)
    totals, (results, input_grads) = lax.scan(one_sequence, zeros_start, (inputs, slot_tags, backs))
    return (results.reshape(TOKENS, D).astype(jnp.bfloat16), input_grads.reshape(TOKENS, D), totals[0], totals[1], totals[2], totals[3], totals[4], totals[5], totals[6], totals[7], totals[8], totals[9], totals[10], totals[11], totals[12], totals[13], totals[14])
```

```python
from functools import partial, reduce
import math

import jax
import jax.numpy as jnp
from jax import lax
from jax.experimental import pallas as pl
from jax.experimental.pallas import tpu as pltpu
from jax.sharding import PartitionSpec as P

HEAD_DIM = 48
SEG0 = 1024
BRANCHES = 5


EPSILON = 1e-05
MASKED = -1000000000.0
GELU_SCALE = 0.7978845608028654
F32 = jnp.float32
BF16 = jnp.bfloat16
HEADS_HERE = 8
QKV = 3 * HEAD_DIM
AUG = 16
OUT_ROWS = HEAD_DIM + AUG
NT = (((1,), (1,)), ((), ()))
TN = (((0,), (0,)), ((), ()))


def partner(value, axis, bit):
    mask = 2**bit
    pairs = [(source, source ^ mask) for source in range(lax.axis_size(axis))]
    return lax.ppermute(value, axis, pairs)


def layer_norm(values, norm_gain, norm_shift):
    row_mean = jnp.mean(values, axis=-1, keepdims=True)
    centred = values - row_mean
    row_var = jnp.mean(centred * centred, axis=-1, keepdims=True)
    return centred * lax.rsqrt(row_var + EPSILON) * norm_gain + norm_shift


def gelu_tanh(values):
    cubic = values + 0.044715 * values * values * values
    return 0.5 * values * (1.0 + jnp.tanh(GELU_SCALE * cubic))


def pick_rows(values, stride, offsets):
    count = offsets.shape[0]
    shaped = values.reshape((values.shape[0] // stride, stride) + values.shape[1:])
    chosen_mask = (jnp.arange(stride)[:, None] == offsets[None, :]).reshape(
        (1, stride, count) + (1,) * (values.ndim - 2)
    )
    chosen = jnp.sum(
        jnp.where(chosen_mask, shaped, jnp.zeros((), values.dtype)), axis=1, dtype=values.dtype
    )
    return jnp.moveaxis(chosen, 1, 0)


def spread_rows(values, stride, offsets):
    count = offsets.shape[0]
    moved = jnp.moveaxis(values, 0, 1)
    chosen_mask = (jnp.arange(stride)[:, None] == offsets[None, :]).reshape(
        (1, stride, count) + (1,) * (values.ndim - 2)
    )
    full_rows = jnp.where(chosen_mask, moved[:, None], jnp.zeros((), values.dtype))
    return full_rows.reshape((moved.shape[0] * stride,) + moved.shape[1:])


def blockwise(kernel, operands, unit_count, row_count):
    block_size = math.gcd(unit_count, max(1, 512 // row_count))
    split_parts = tuple(
        (item.reshape((unit_count // block_size, block_size) + item.shape[1:]) for item in operands)
    )
    results = lax.map(lambda group_parts: kernel(*group_parts), split_parts)
    return tuple((item.reshape((unit_count,) + item.shape[2:]) for item in results))


def masked_scores(queries, key_units, query_tags, key_tags):
    scores = jnp.einsum("uqd,ukd->uqk", queries, key_units, preferred_element_type=jnp.float32)
    return jnp.where(query_tags[:, :, None] == key_tags[:, None, :], scores, MASKED)


def attend_block(queries, key_units, value_units, query_tags, key_tags):
    scores = masked_scores(queries, key_units, query_tags, key_tags)
    row_peak = jnp.max(scores, axis=-1, keepdims=True)
    weights = jnp.exp(scores - row_peak)
    weight_sum = jnp.sum(weights, axis=-1, keepdims=True)
    attn_probs = (weights / weight_sum).astype(jnp.bfloat16)
    outputs = jnp.einsum(
        "uqk,ukd->uqd", attn_probs, value_units, preferred_element_type=jnp.float32
    )
    return (outputs, row_peak[..., 0] + jnp.log(weight_sum[..., 0]))


def both_grads_block(
    queries, key_units, value_units, query_tags, key_tags, log_total, out_grad, lse_grad
):
    attn_probs = jnp.exp(
        masked_scores(queries, key_units, query_tags, key_tags) - log_total[:, :, None]
    )
    prob_grad = jnp.einsum(
        "uqd,ukd->uqk", out_grad, value_units, preferred_element_type=jnp.float32
    )
    inner_sum = jnp.sum(attn_probs * prob_grad, axis=-1, keepdims=True)
    score_grad = (attn_probs * (prob_grad - inner_sum + lse_grad[:, :, None])).astype(jnp.bfloat16)
    query_grad = jnp.einsum(
        "uqk,ukd->uqd", score_grad, key_units, preferred_element_type=jnp.float32
    )
    key_grad = jnp.einsum("uqk,uqd->ukd", score_grad, queries, preferred_element_type=jnp.float32)
    value_grad = jnp.einsum(
        "uqk,uqd->ukd",
        attn_probs.astype(jnp.bfloat16),
        out_grad,
        preferred_element_type=jnp.float32,
    )
    return (query_grad, key_grad, value_grad)


def double_up(blocks, levels, row_pos, sender):
    blocks = list(blocks)
    for bit_level in range(max(levels)):
        active = [member for member in range(len(blocks)) if levels[member] > bit_level]
        lengths = [blocks[member].shape[2] for member in active]
        joined = jnp.concatenate([blocks[member] for member in active], axis=2)
        received = sender(joined, bit_level)
        upper_half = row_pos >> bit_level & 1 == 1
        offset_at = 0
        for member, length in zip(active, lengths):
            theirs = lax.slice_in_dim(received, offset_at, offset_at + length, axis=2)
            own_part = blocks[member]
            blocks[member] = jnp.where(
                upper_half,
                jnp.concatenate([theirs, own_part], axis=2),
                jnp.concatenate([own_part, theirs], axis=2),
            )
            offset_at += length
    return blocks


def halve_down(blocks, levels, row_pos, sender):
    blocks = list(blocks)
    for bit_level in reversed(range(max(levels))):
        active = [member for member in range(len(blocks)) if levels[member] > bit_level]
        upper_half = row_pos >> bit_level & 1 == 1
        kept_parts = []
        sent_parts = []
        for member in active:
            half_len = blocks[member].shape[2] // 2
            lower_part = blocks[member][:, :, :half_len]
            upper_part = blocks[member][:, :, half_len:]
            kept_parts.append(jnp.where(upper_half, upper_part, lower_part))
            sent_parts.append(jnp.where(upper_half, lower_part, upper_part))
        received = sender(jnp.concatenate(sent_parts, axis=2), bit_level)
        offset_at = 0
        for member, kept_part in zip(active, kept_parts):
            length = kept_part.shape[2]
            blocks[member] = kept_part + lax.slice_in_dim(
                received, offset_at, offset_at + length, axis=2
            )
            offset_at += length
    return blocks


def local_general(
    tokens,
    doc_ids,
    valid,
    ln1_gain,
    ln1_shift,
    w_query,
    b_query,
    w_key,
    w_value,
    b_value,
    w_out,
    b_out,
    ln2_gain,
    ln2_shift,
    w_up,
    b_up,
    w_down,
    b_down,
    cotangent,
):
    rows_here = tokens.shape[0]
    local_width = w_query.shape[1]
    heads_here = local_width // HEAD_DIM
    scaling = HEAD_DIM ** (-0.5)
    unit_pos = lax.axis_index("unit")
    row_pos = lax.axis_index("row")
    head_ids = unit_pos * heads_here + jnp.arange(heads_here, dtype=jnp.int32)
    all_tags = jnp.where(valid == 1, doc_ids, -1).reshape(-1)
    own_tags = lax.dynamic_slice_in_dim(all_tags, row_pos * rows_here, rows_here)
    residual = tokens.astype(jnp.float32)
    normed = layer_norm(residual, ln1_gain, ln1_shift)
    normed_low = normed.astype(jnp.bfloat16)
    head_shape = (rows_here, heads_here, HEAD_DIM)
    query_all = (
        ((jnp.dot(normed_low, w_query, preferred_element_type=jnp.float32) + b_query) * scaling)
        .astype(jnp.bfloat16)
        .reshape(head_shape)
    )
    key_all = (
        jnp.dot(normed_low, w_key, preferred_element_type=jnp.float32)
        .astype(jnp.bfloat16)
        .reshape(head_shape)
    )
    value_all = (
        (jnp.dot(normed_low, w_value, preferred_element_type=jnp.float32) + b_value)
        .astype(jnp.bfloat16)
        .reshape(head_shape)
    )
    branch_plans = []
    for branch in range(BRANCHES):
        stride = 2**branch
        extent = SEG0 * stride
        group_size = max(1, extent // rows_here)
        branch_plans.append(
            (
                stride,
                group_size,
                group_size.bit_length() - 1,
                max(1, rows_here // extent),
                head_ids % stride,
            )
        )
    levels = [branch_plan[2] for branch_plan in branch_plans]
    local_kv = [
        jnp.stack(
            [
                pick_rows(key_all, branch_plan[0], branch_plan[4]),
                pick_rows(value_all, branch_plan[0], branch_plan[4]),
            ]
        )
        for branch_plan in branch_plans
    ]

    def send_pairs(joined, bit_level):
        return partner(joined, "row", bit_level)

    gathered = double_up(local_kv, levels, row_pos, send_pairs)
    saved_parts = []
    branch_outs = []
    branch_lses = []
    selections = []
    for branch in range(BRANCHES):
        stride, group_size, branch_levels, segments, offsets = branch_plans[branch]
        unit_count = heads_here * segments
        per_unit = rows_here // stride // segments
        block_start = row_pos // group_size * (group_size * rows_here)
        block_tags = lax.dynamic_slice_in_dim(all_tags, block_start, group_size * rows_here)
        key_tags = pick_rows(
            jnp.broadcast_to(block_tags[:, None], (group_size * rows_here, heads_here)),
            stride,
            offsets,
        )
        query_tags = pick_rows(
            jnp.broadcast_to(own_tags[:, None], (rows_here, heads_here)), stride, offsets
        )
        queries = pick_rows(query_all, stride, offsets)
        key_units = gathered[branch][0]
        value_units = gathered[branch][1]
        outputs, log_total = blockwise(
            attend_block,
            (queries, key_units, value_units, query_tags, key_tags),
            unit_count,
            per_unit,
        )
        saved_parts.append((queries, key_units, value_units, query_tags, key_tags, log_total))
        branch_outs.append(spread_rows(outputs, stride, offsets))
        branch_lses.append(spread_rows(log_total, stride, offsets))
        selections.append(jnp.arange(rows_here)[:, None] % stride == offsets[None, :])
    peak_lse = reduce(
        jnp.maximum,
        [
            jnp.where(mask_here, lse_here, MASKED)
            for mask_here, lse_here in zip(selections, branch_lses)
        ],
    )
    weights = [
        jnp.where(mask_here, jnp.exp(jnp.where(mask_here, lse_here, peak_lse) - peak_lse), 0.0)
        for mask_here, lse_here in zip(selections, branch_lses)
    ]
    weight_sum = reduce(jnp.add, weights)
    shares = [weight_here / weight_sum for weight_here in weights]
    merged = reduce(
        jnp.add,
        [share_here[:, :, None] * out_here for share_here, out_here in zip(shares, branch_outs)],
    )
    merged_low = merged.reshape(rows_here, local_width).astype(jnp.bfloat16)
    attention = (
        lax.psum(jnp.dot(merged_low, w_out, preferred_element_type=jnp.float32), "unit") + b_out
    )
    middle = residual + attention
    normed2 = layer_norm(middle, ln2_gain, ln2_shift)
    normed2_low = normed2.astype(jnp.bfloat16)
    up_input = jnp.dot(normed2_low, w_up, preferred_element_type=jnp.float32) + b_up
    hidden_low = gelu_tanh(up_input).astype(jnp.bfloat16)
    feed_out = (
        lax.psum(jnp.dot(hidden_low, w_down, preferred_element_type=jnp.float32), "unit") + b_down
    )
    mixed_out = (middle + feed_out).astype(jnp.bfloat16)
    back_rows = cotangent.astype(jnp.float32)
    grad_b_down = jnp.sum(back_rows, axis=0)
    grad_w_down = jnp.einsum("tf,td->fd", hidden_low, cotangent, preferred_element_type=jnp.float32)
    hidden_grad = jnp.einsum("td,fd->tf", cotangent, w_down, preferred_element_type=jnp.float32)
    _, gelu_pull = jax.vjp(gelu_tanh, up_input)
    up_grad_low = gelu_pull(hidden_grad)[0].astype(jnp.bfloat16)
    grad_b_up = jnp.sum(up_grad_low.astype(jnp.float32), axis=0)
    grad_w_up = jnp.einsum(
        "tc,tf->cf", normed2_low, up_grad_low, preferred_element_type=jnp.float32
    )
    normed2_grad = lax.psum(
        jnp.einsum("tf,cf->tc", up_grad_low, w_up, preferred_element_type=jnp.float32), "unit"
    )
    _, norm2_pull = jax.vjp(layer_norm, middle, ln2_gain, ln2_shift)
    middle_part, grad_ln2_gain, grad_ln2_shift = norm2_pull(normed2_grad)
    middle_grad = back_rows + middle_part
    attention_grad = middle_grad.astype(jnp.bfloat16)
    grad_b_out = jnp.sum(attention_grad.astype(jnp.float32), axis=0)
    grad_w_out = jnp.einsum(
        "tc,td->cd", merged_low, attention_grad, preferred_element_type=jnp.float32
    )
    merged_grad = jnp.einsum(
        "td,cd->tc", attention_grad, w_out, preferred_element_type=jnp.float32
    ).reshape(head_shape)
    share_grads = [jnp.sum(merged_grad * out_here, axis=-1) for out_here in branch_outs]
    mean_grad = reduce(
        jnp.add, [share_here * grad_here for share_here, grad_here in zip(shares, share_grads)]
    )
    out_grad_units = []
    lse_grad_units = []
    for branch in range(BRANCHES):
        stride, group_size, branch_levels, segments, offsets = branch_plans[branch]
        unit_count = heads_here * segments
        per_unit = rows_here // stride // segments
        out_grad_rows = (shares[branch][:, :, None] * merged_grad).astype(jnp.bfloat16)
        lse_grad_rows = shares[branch] * (share_grads[branch] - mean_grad)
        out_grad_units.append(pick_rows(out_grad_rows, stride, offsets))
        lse_grad_units.append(pick_rows(lse_grad_rows, stride, offsets))
    query_grad = jnp.zeros(head_shape, jnp.float32)
    key_grad = jnp.zeros(head_shape, jnp.float32)
    value_grad = jnp.zeros(head_shape, jnp.float32)
    returned = []
    for branch in range(BRANCHES):
        stride, group_size, branch_levels, segments, offsets = branch_plans[branch]
        unit_count = heads_here * segments
        per_unit = rows_here // stride // segments
        queries, key_units, value_units, query_tags, key_tags, log_total = saved_parts[branch]
        grad_q, grad_k, grad_v = blockwise(
            both_grads_block,
            (
                queries,
                key_units,
                value_units,
                query_tags,
                key_tags,
                log_total,
                out_grad_units[branch],
                lse_grad_units[branch],
            ),
            unit_count,
            per_unit,
        )
        query_grad = query_grad + spread_rows(grad_q, stride, offsets)
        returned.append(jnp.stack([grad_k, grad_v]))

    def send_grads(joined, bit_level):
        return partner(joined, "row", bit_level)

    returned = halve_down(returned, levels, row_pos, send_grads)
    for branch in range(BRANCHES):
        stride, group_size, branch_levels, segments, offsets = branch_plans[branch]
        key_grad = key_grad + spread_rows(returned[branch][0], stride, offsets)
        value_grad = value_grad + spread_rows(returned[branch][1], stride, offsets)
    query_low = query_grad.reshape(rows_here, local_width).astype(jnp.bfloat16)
    key_low = key_grad.reshape(rows_here, local_width).astype(jnp.bfloat16)
    value_low = value_grad.reshape(rows_here, local_width).astype(jnp.bfloat16)
    grad_b_query = scaling * jnp.sum(query_low.astype(jnp.float32), axis=0)
    grad_w_query = scaling * jnp.einsum(
        "tc,tk->ck", normed_low, query_low, preferred_element_type=jnp.float32
    )
    grad_w_key = jnp.einsum("tc,tk->ck", normed_low, key_low, preferred_element_type=jnp.float32)
    grad_w_value = jnp.einsum(
        "tc,tk->ck", normed_low, value_low, preferred_element_type=jnp.float32
    )
    grad_b_value = jnp.sum(value_low.astype(jnp.float32), axis=0)
    normed_part = (
        scaling * jnp.einsum("tk,ck->tc", query_low, w_query, preferred_element_type=jnp.float32)
        + jnp.einsum("tk,ck->tc", key_low, w_key, preferred_element_type=jnp.float32)
        + jnp.einsum("tk,ck->tc", value_low, w_value, preferred_element_type=jnp.float32)
    )
    normed_grad = lax.psum(normed_part, "unit")
    _, norm1_pull = jax.vjp(layer_norm, residual, ln1_gain, ln1_shift)
    input_part, grad_ln1_gain, grad_ln1_shift = norm1_pull(normed_grad)
    grad_tokens = middle_grad + input_part
    (
        grad_ln1_gain,
        grad_ln1_shift,
        grad_w_query,
        grad_b_query,
        grad_w_key,
        grad_w_value,
        grad_b_value,
        grad_w_out,
        grad_b_out,
        grad_ln2_gain,
        grad_ln2_shift,
        grad_w_up,
        grad_b_up,
        grad_w_down,
        grad_b_down,
    ) = lax.psum(
        (
            grad_ln1_gain,
            grad_ln1_shift,
            grad_w_query,
            grad_b_query,
            grad_w_key,
            grad_w_value,
            grad_b_value,
            grad_w_out,
            grad_b_out,
            grad_ln2_gain,
            grad_ln2_shift,
            grad_w_up,
            grad_b_up,
            grad_w_down,
            grad_b_down,
        ),
        "row",
    )
    return (
        mixed_out,
        grad_tokens,
        grad_ln1_gain,
        grad_ln1_shift,
        grad_w_query,
        grad_b_query,
        grad_w_key,
        grad_w_value,
        grad_b_value,
        grad_w_out,
        grad_b_out,
        grad_ln2_gain,
        grad_ln2_shift,
        grad_w_up,
        grad_b_up,
        grad_w_down,
        grad_b_down,
    )


def bitrev(value, bits):
    return sum((value >> at & 1) << (bits - 1 - at) for at in range(bits))


def class_lanes(head, branch):
    size = SEG0 >> branch
    start = bitrev(head % 2**branch, branch) * size
    return slice(start, start + size)


LANES0 = {1: (0, 512), 2: (512, 256), 3: (768, 128), 4: (896, 64)}
LANES1 = {2: (0, 512), 3: (512, 256), 4: (768, 128)}
LANES2 = {3: (0, 512), 4: (512, 256)}


def one_hot_rows(forward):
    row = lax.broadcasted_iota(jnp.int32, (SEG0, SEG0), 0)
    col = lax.broadcasted_iota(jnp.int32, (SEG0, SEG0), 1)
    place, slot = (row, col) if forward else (col, row)
    group = place // 64
    rev = (group & 1) * 8 + (group >> 1 & 1) * 4 + (group >> 2 & 1) * 2 + (group >> 3 & 1)
    return jnp.where(rev + 16 * (place % 64) == slot, 1.0, 0.0).astype(BF16)


def split_three(value):
    high = value.astype(BF16).astype(F32)
    rest = value - high
    mid = rest.astype(BF16).astype(F32)
    return high, mid, rest - mid


def rows_iota(count, lanes):
    return lax.broadcasted_iota(jnp.int32, (count, lanes), 0)


def project_kernel(
    pos_ref, tok_ref, gain_ref, shift_ref, wq_ref, bq_ref, wk_ref, wv_ref, bv_ref, all_ref, send_ref, normed_ref
):
    dl = pos_ref[0]
    unit = pos_ref[1]
    values = tok_ref[...].astype(F32)
    centred = values - jnp.mean(values, axis=-1, keepdims=True)
    row_var = jnp.mean(centred * centred, axis=-1, keepdims=True)
    normed = (centred * lax.rsqrt(row_var + EPSILON) * gain_ref[...] + shift_ref[...]).astype(BF16)
    order = one_hot_rows(False)
    normed_t = lax.dot_general(normed, order, TN, preferred_element_type=F32).astype(BF16)
    normed_ref[...] = normed_t

    def project(w_ref):
        return lax.dot_general(w_ref[...], normed_t, TN, preferred_element_type=F32)

    query = ((project(wq_ref) + bq_ref[...]) * HEAD_DIM**-0.5).astype(BF16)
    key = project(wk_ref).astype(BF16)
    value = (project(wv_ref) + bv_ref[...]).astype(BF16)
    for head in range(HEADS_HERE):
        own = slice(head * HEAD_DIM, (head + 1) * HEAD_DIM)
        for at, part in enumerate((query, key, value)):
            rows = slice(at * HEAD_DIM, (at + 1) * HEAD_DIM)
            here = part[own]
            all_ref[head, rows, :] = here
            for branch in (1, 2, 3):
                start, size = LANES0[branch]
                send_ref[head ^ dl, rows, start : start + size] = here[:, class_lanes(head, branch)]
            both = here[:, class_lanes(head, 3)]
            picked = jnp.where(unit == 0, both[:, :64].astype(F32), both[:, 64:].astype(F32))
            send_ref[head ^ dl, rows, 896:960] = picked.astype(BF16)
            send_ref[head ^ dl, rows, 960:1024] = jnp.zeros((HEAD_DIM, 64), BF16)


def whole_spec(shape):
    return pl.BlockSpec(shape, lambda *_: (0,) * len(shape))


def project_call(place, tokens, gain, shift, w_query, b_query, w_key, w_value, b_value):
    width = HEADS_HERE * HEAD_DIM
    model = tokens.shape[1]
    args = (tokens, gain[None], shift[None], w_query, b_query[:, None], w_key, w_value, b_value[:, None])
    out_shape = [
        jax.ShapeDtypeStruct((HEADS_HERE, QKV, SEG0), BF16),
        jax.ShapeDtypeStruct((HEADS_HERE, QKV, SEG0), BF16),
        jax.ShapeDtypeStruct((model, SEG0), BF16),
    ]
    return pl.pallas_call(
        project_kernel,
        grid_spec=pltpu.PrefetchScalarGridSpec(
            num_scalar_prefetch=1,
            grid=(1,),
            in_specs=[whole_spec(a.shape) for a in args],
            out_specs=[whole_spec(o.shape) for o in out_shape],
        ),
        out_shape=out_shape,
        name="project",
        cost_estimate=pl.CostEstimate(
            flops=2 * SEG0 * model * (3 * width + SEG0), bytes_accessed=12 * 2**20, transcendentals=SEG0
        ),
    )(place, *args)


def key_tail(tags):
    at = rows_iota(AUG, tags.shape[1])
    return jnp.where((at == tags) | (at > 12), 1.0, 0.0).astype(BF16)


def query_tail(tags):
    at = rows_iota(AUG, tags.shape[1])
    return jnp.where((at == tags) | (at > 12), 0.0, MASKED)


def gather_rows(pieces, rows):
    return jnp.concatenate([ref[0, rows[0] : rows[1], :size] for ref, size in pieces], axis=1)


def forward_kernel(*refs, sizes, tile, packed):
    count = len(sizes)
    piece_refs, (tag_ref,) = refs[:count], refs[count : count + 1]
    outs = refs[count + 1 :]
    shared = count if len(sizes) < 5 else count - 1
    q_pieces = [(piece_refs[i], sizes[i]) for i in range(shared)]
    kv_pieces = q_pieces
    query = gather_rows(q_pieces, (0, HEAD_DIM))
    key = gather_rows(kv_pieces, (HEAD_DIM, 2 * HEAD_DIM))
    value = gather_rows(kv_pieces, (2 * HEAD_DIM, QKV))
    if shared < count:
        last = piece_refs[-1]
        key = jnp.concatenate([key, last[0, :HEAD_DIM, :]], axis=1)
        value = jnp.concatenate([value, last[0, HEAD_DIM : 2 * HEAD_DIM, :]], axis=1)
    tags = tag_ref[0]
    keys = key.shape[1]
    key_rows = jnp.concatenate([key, key_tail(tags)], axis=0).T
    ones = jnp.where(rows_iota(AUG, keys) == 0, 1.0, 0.0).astype(BF16)
    value_aug = jnp.concatenate([value, ones], axis=0)
    query_aug = jnp.concatenate([query, query_tail(tags[:, : query.shape[1]]).astype(BF16)], axis=0)
    for start in range(0, query.shape[1], tile):
        lanes = slice(start, start + tile)
        scores = jnp.dot(key_rows, query_aug[:, lanes], preferred_element_type=F32)
        peak = jnp.max(scores, axis=0, keepdims=True)
        weights = jnp.exp(scores - peak).astype(BF16)
        summed = jnp.dot(value_aug, weights, preferred_element_type=F32)
        total = summed[HEAD_DIM : HEAD_DIM + 1]
        outputs = summed[:HEAD_DIM] / total
        lse = peak + jnp.log(total)
        if packed:
            (o_ref,) = outs
            o_ref[0, :HEAD_DIM, lanes] = outputs.astype(BF16)
            high, mid, low = split_three(lse)
            at = rows_iota(AUG, tile)
            tail = jnp.where(at == 0, high, jnp.where(at == 1, mid, jnp.where(at == 2, low, 0.0)))
            o_ref[0, HEAD_DIM:, lanes] = tail.astype(BF16)
        else:
            o_ref, lse_ref = outs
            o_ref[0, :, lanes] = outputs
            lse_ref[0, :, lanes] = lse


def backward_kernel(*refs, sizes, grad_sizes, tile, out_type):
    count, grads = len(sizes), len(grad_sizes)
    piece_refs = refs[:count]
    grad_refs = refs[count : count + grads]
    tag_ref, out_ref = refs[count + grads : count + grads + 2]
    kv_out_ref = refs[-1]
    shared = count if count < 5 else count - 1
    pieces = [(piece_refs[i], sizes[i]) for i in range(shared)]
    query = gather_rows(pieces, (0, HEAD_DIM))
    key = gather_rows(pieces, (HEAD_DIM, 2 * HEAD_DIM))
    value = gather_rows(pieces, (2 * HEAD_DIM, QKV))
    if shared < count:
        last = piece_refs[-1]
        key = jnp.concatenate([key, last[0, :HEAD_DIM, :]], axis=1)
        value = jnp.concatenate([value, last[0, HEAD_DIM : 2 * HEAD_DIM, :]], axis=1)
    grad_pieces = [(grad_refs[i], grad_sizes[i]) for i in range(grads)]
    grad = gather_rows(grad_pieces, (0, HEAD_DIM))
    tail = gather_rows(grad_pieces, (HEAD_DIM, OUT_ROWS)).astype(F32)
    tags = tag_ref[0]
    keys, queries = key.shape[1], query.shape[1]
    key_rows = jnp.concatenate([key, key_tail(tags)], axis=0).T
    ones = jnp.where(rows_iota(AUG, keys) < 3, 1.0, 0.0).astype(BF16)
    value_rows = jnp.concatenate([value, ones], axis=0).T
    at = rows_iota(AUG, queries)
    mask = query_tail(tags[:, :queries])
    query_aug = jnp.concatenate([query, jnp.where(at > 12, tail, mask).astype(BF16)], axis=0)
    grad_aug = jnp.concatenate([grad, jnp.where(at < 3, tail, 0.0).astype(BF16)], axis=0)
    key_grad = jnp.zeros((HEAD_DIM, keys), F32)
    value_grad = jnp.zeros((HEAD_DIM, keys), F32)
    for start in range(0, queries, tile):
        lanes = slice(start, start + tile)
        probs = jnp.exp(jnp.dot(key_rows, query_aug[:, lanes], preferred_element_type=F32))
        prob_grad = jnp.dot(value_rows, grad_aug[:, lanes], preferred_element_type=F32)
        score_grad = (probs * prob_grad).astype(BF16)
        probs_low = probs.astype(BF16)
        out_ref[0, :HEAD_DIM, lanes] = jnp.dot(key, score_grad, preferred_element_type=F32).astype(out_type)
        key_grad = key_grad + lax.dot_general(query[:, lanes], score_grad, NT, preferred_element_type=F32)
        value_grad = value_grad + lax.dot_general(grad[:, lanes], probs_low, NT, preferred_element_type=F32)
    if shared < count:
        half = keys // 2
        out_ref[0, HEAD_DIM : 2 * HEAD_DIM, :] = key_grad[:, :half].astype(out_type)
        out_ref[0, 2 * HEAD_DIM :, :] = value_grad[:, :half].astype(out_type)
        kv_out_ref[0, :HEAD_DIM, :] = key_grad[:, half:].astype(out_type)
        kv_out_ref[0, HEAD_DIM:, :] = value_grad[:, half:].astype(out_type)
    else:
        out_ref[0, HEAD_DIM : 2 * HEAD_DIM, :] = key_grad.astype(out_type)
        out_ref[0, 2 * HEAD_DIM :, :] = value_grad.astype(out_type)


def lane_spec(rows, start, size):
    block = max(size, 128)
    return pl.BlockSpec((1, rows, block), lambda head, at=start // block: (head, 0, at))


def branch_pieces(branch, parts):
    if branch == 0:
        return [(parts[0], 0, SEG0)]
    pieces = [(parts[0],) + LANES0[branch], (parts[1],) + LANES0[branch]]
    if branch > 1:
        pieces.append((parts[2],) + LANES1[branch])
    if branch > 2:
        pieces.append((parts[3],) + LANES2[branch])
    return pieces


def forward_call(branch, parts, tags):
    pieces = branch_pieces(branch, parts)
    queries = sum(piece[2] for piece in pieces)
    if branch == 4:
        pieces.append((parts[4], 0, 512))
    heads = 8 >> min(branch, 3)
    packed = branch > 0
    if packed:
        out_shape = [jax.ShapeDtypeStruct((heads, OUT_ROWS, queries), BF16)]
        out_specs = [pl.BlockSpec((1, OUT_ROWS, queries), lambda head: (head, 0, 0))]
    else:
        out_shape = [
            jax.ShapeDtypeStruct((heads, HEAD_DIM, queries), F32),
            jax.ShapeDtypeStruct((heads, 1, queries), F32),
        ]
        out_specs = [
            pl.BlockSpec((1, HEAD_DIM, queries), lambda head: (head, 0, 0)),
            pl.BlockSpec((1, 1, queries), lambda head: (head, 0, 0)),
        ]
    return pl.pallas_call(
        partial(forward_kernel, sizes=tuple(piece[2] for piece in pieces), tile=512, packed=packed),
        grid=(heads,),
        in_specs=[lane_spec(array.shape[1], start, size) for array, start, size in pieces]
        + [pl.BlockSpec((1, 1, SEG0), lambda head: (head, 0, 0))],
        out_specs=out_specs,
        out_shape=out_shape,
        name=f"attend{branch}",
        cost_estimate=pl.CostEstimate(
            flops=heads * queries * SEG0 * 2 * 512, bytes_accessed=heads * SEG0 * 512, transcendentals=heads * queries * SEG0
        ),
    )(*[piece[0] for piece in pieces], tags)


def backward_call(branch, parts, grad_parts, tags):
    pieces = branch_pieces(branch, parts)
    grad_pieces = branch_pieces(branch, grad_parts)
    queries = sum(piece[2] for piece in pieces)
    heads = 8 >> min(branch, 3)
    out_type = F32 if branch == 0 else BF16
    out_shape = [jax.ShapeDtypeStruct((heads, QKV, queries), out_type)]
    if branch == 4:
        pieces.append((parts[4], 0, 512))
        out_shape.append(jax.ShapeDtypeStruct((heads, 2 * HEAD_DIM, 512), out_type))
    return pl.pallas_call(
        partial(
            backward_kernel,
            sizes=tuple(piece[2] for piece in pieces),
            grad_sizes=tuple(piece[2] for piece in grad_pieces),
            tile=512,
            out_type=out_type,
        ),
        grid=(heads,),
        in_specs=[lane_spec(array.shape[1], start, size) for array, start, size in pieces + grad_pieces]
        + [pl.BlockSpec((1, 1, SEG0), lambda head: (head, 0, 0))],
        out_specs=[pl.BlockSpec((1,) + out.shape[1:], lambda head: (head, 0, 0)) for out in out_shape],
        out_shape=out_shape,
        name=f"attend_back{branch}",
        cost_estimate=pl.CostEstimate(
            flops=heads * queries * SEG0 * 2 * 768, bytes_accessed=heads * SEG0 * 1024, transcendentals=heads * queries * SEG0
        ),
    )(*[piece[0] for piece in pieces + grad_pieces], tags)


def branch_blocks(head, unit, ref, rows, at):
    blocks = []
    for branch in (1, 2, 3):
        start, size = LANES0[branch]
        blocks.append((class_lanes(head, branch), ref[at, rows[0] : rows[1], start : start + size].astype(F32)))
    last = ref[at, rows[0] : rows[1], 896:960].astype(F32)
    twice = jnp.concatenate([last, last], axis=1)
    lane = lax.broadcasted_iota(jnp.int32, twice.shape, 1)
    blocks.append((class_lanes(head, 3), twice, (lane >= 64) == (unit == 1)))
    return blocks


def merge_kernel(pos_ref, o_ref, lse_ref, back_ref, merged_ref, total_ref):
    dl = pos_ref[0]
    unit = pos_ref[1]
    for head in range(HEADS_HERE):
        at = head ^ dl
        peak = lse_ref[head]
        tails = branch_blocks(head, unit, back_ref, (HEAD_DIM, OUT_ROWS), at)
        lses = []
        for block in tails:
            value = block[1][0:1] + block[1][1:2] + block[1][2:3]
            if len(block) == 3:
                value = jnp.where(block[2][0:1], value, MASKED)
            lses.append((block[0], value))
        full = [lse_ref[head]]
        for lanes, value in lses:
            pad = []
            if lanes.start:
                pad.append(jnp.full((1, lanes.start), MASKED, F32))
            pad.append(value)
            if lanes.stop < SEG0:
                pad.append(jnp.full((1, SEG0 - lanes.stop), MASKED, F32))
            full.append(jnp.concatenate(pad, axis=1))
        peak = reduce(jnp.maximum, full)
        weights = [jnp.exp(value - peak) for value in full]
        summed = reduce(jnp.add, weights)
        total_ref[head] = peak + jnp.log(summed)
        shares = [weight / summed for weight in weights]
        rows = slice(head * HEAD_DIM, (head + 1) * HEAD_DIM)
        merged_ref[rows, :] = o_ref[head] * shares[0]
        outs = branch_blocks(head, unit, back_ref, (0, HEAD_DIM), at)
        for block, share in zip(outs, shares[1:]):
            merged_ref[rows, block[0]] += block[1] * share[:, block[0]]


def merge_call(place, outputs, lse, back):
    width = HEADS_HERE * HEAD_DIM
    out_shape = [jax.ShapeDtypeStruct((width, SEG0), F32), jax.ShapeDtypeStruct((HEADS_HERE, 1, SEG0), F32)]
    args = (outputs, lse, back)
    return pl.pallas_call(
        merge_kernel,
        grid_spec=pltpu.PrefetchScalarGridSpec(
            num_scalar_prefetch=1,
            grid=(1,),
            in_specs=[whole_spec(a.shape) for a in args],
            out_specs=[whole_spec(o.shape) for o in out_shape],
        ),
        out_shape=out_shape,
        name="merge",
        cost_estimate=pl.CostEstimate(flops=10**8, bytes_accessed=6 * 2**20, transcendentals=SEG0 * 8),
    )(place, *args)


def spread_kernel(pos_ref, grad_ref, merged_ref, total_ref, all_ref, send_ref):
    dl = pos_ref[0]
    unit = pos_ref[1]
    at = rows_iota(AUG, SEG0)
    for head in range(HEADS_HERE):
        rows = slice(head * HEAD_DIM, (head + 1) * HEAD_DIM)
        grad = grad_ref[rows, :]
        delta = jnp.sum(grad.astype(F32) * merged_ref[rows, :], axis=0, keepdims=True)
        parts = split_three(-delta) + split_three(-total_ref[head])
        tail = jnp.zeros((AUG, SEG0), F32)
        for row, part in zip((0, 1, 2, 13, 14, 15), parts):
            tail = jnp.where(at == row, part, tail)
        for place, here in ((slice(0, HEAD_DIM), grad), (slice(HEAD_DIM, OUT_ROWS), tail.astype(BF16))):
            all_ref[head, place, :] = here
            for branch in (1, 2, 3):
                start, size = LANES0[branch]
                send_ref[head ^ dl, place, start : start + size] = here[:, class_lanes(head, branch)]
            both = here[:, class_lanes(head, 3)]
            picked = jnp.where(unit == 0, both[:, :64].astype(F32), both[:, 64:].astype(F32))
            send_ref[head ^ dl, place, 896:960] = picked.astype(BF16)
            send_ref[head ^ dl, place, 960:1024] = jnp.zeros((here.shape[0], 64), BF16)


def spread_call(place, grad, merged, total):
    out_shape = [jax.ShapeDtypeStruct((HEADS_HERE, OUT_ROWS, SEG0), BF16)] * 2
    args = (grad, merged, total)
    return pl.pallas_call(
        spread_kernel,
        grid_spec=pltpu.PrefetchScalarGridSpec(
            num_scalar_prefetch=1,
            grid=(1,),
            in_specs=[whole_spec(a.shape) for a in args],
            out_specs=[whole_spec(o.shape) for o in out_shape],
        ),
        out_shape=out_shape,
        name="spread",
        cost_estimate=pl.CostEstimate(flops=10**8, bytes_accessed=5 * 2**20, transcendentals=0),
    )(place, *args)


def collect_kernel(pos_ref, own_ref, back_ref, out_ref, sum_ref):
    dl = pos_ref[0]
    unit = pos_ref[1]
    width = HEADS_HERE * HEAD_DIM
    for head in range(HEADS_HERE):
        sum_ref[...] = own_ref[head]
        for block in branch_blocks(head, unit, back_ref, (0, QKV), head ^ dl):
            value = block[1] if len(block) == 2 else jnp.where(block[2], block[1], 0.0)
            sum_ref[:, block[0]] += value
        for at in range(3):
            out_ref[at * width + head * HEAD_DIM : at * width + (head + 1) * HEAD_DIM, :] = sum_ref[
                at * HEAD_DIM : (at + 1) * HEAD_DIM, :
            ].astype(BF16)


def collect_call(place, own, back):
    out_shape = jax.ShapeDtypeStruct((HEADS_HERE * QKV, SEG0), BF16)
    args = (own, back)
    return pl.pallas_call(
        collect_kernel,
        grid_spec=pltpu.PrefetchScalarGridSpec(
            num_scalar_prefetch=1,
            grid=(1,),
            in_specs=[whole_spec(a.shape) for a in args],
            out_specs=whole_spec(out_shape.shape),
            scratch_shapes=[pltpu.VMEM((QKV, SEG0), F32)],
        ),
        out_shape=out_shape,
        name="collect",
        cost_estimate=pl.CostEstimate(flops=10**8, bytes_accessed=9 * 2**20, transcendentals=0),
    )(place, *args)


def swap_unit(value):
    return lax.ppermute(value, "unit", [(0, 1), (1, 0)])


def cat(*parts):
    return jnp.concatenate(parts, axis=2)


def step1_rows(own, first):
    return cat(
        *[array[2:4, :, start : start + size] for start, size in (LANES0[2], LANES0[3], LANES0[4]) for array in (own, first)]
    )


def step2_rows(own, first, second):
    pieces = []
    for branch in (3, 4):
        for array in (own, first):
            start, size = LANES0[branch]
            pieces.append(array[1:2, :, start : start + size])
        start, size = LANES1[branch]
        pieces.append(second[1:2, :, start : start + size])
    return cat(*pieces)


def step3_rows(own, first, second, third):
    rows = slice(HEAD_DIM, QKV)
    return cat(
        own[0:1, rows, 896:960], first[0:1, rows, 896:960], second[0:1, rows, 768:896], third[0:1, rows, 512:768]
    )


def send_down(own, copy_last):
    first = partner(own[4:8, :, :960], "row", 0)
    second = partner(step1_rows(own, first), "row", 1)
    third = partner(step2_rows(own, first, second), "row", 2)
    parts = [own, first, second, third]
    if copy_last:
        parts.append(partner(step3_rows(*parts), "row", 3))
    return parts


def send_up(out1, out2, out3, out4):
    third = partner(cat(out3[:, :, 512:1024], out4[:, :, 256:512]), "row", 2)

    def joined(low, high):
        return jnp.concatenate([low, high], axis=0)

    second = partner(
        cat(
            out2[:, :, 512:1024],
            joined(out3[:, :, 256:512], third[:, :, 256:512]),
            joined(out4[:, :, 128:256], third[:, :, 640:768]),
        ),
        "row",
        1,
    )

    def rows_of(at):
        return cat(
            out1[:, :, 512 * at : 512 * at + 512],
            joined(out2[:, :, 256 * at : 256 * at + 256], second[:, :, 256 * at : 256 * at + 256]),
            jnp.concatenate(
                [
                    out3[:, :, 128 * at : 128 * at + 128],
                    third[:, :, 128 * at : 128 * at + 128],
                    second[:, :, 512 + 128 * at : 640 + 128 * at],
                ],
                axis=0,
            ),
            jnp.concatenate(
                [
                    out4[:, :, 64 * at : 64 * at + 64],
                    third[:, :, 512 + 64 * at : 576 + 64 * at],
                    second[:, :, 768 + 64 * at : 832 + 64 * at],
                ],
                axis=0,
            ),
        )

    first = partner(rows_of(1), "row", 0)
    return joined(rows_of(0), first)


def sum_rows(value):
    place = lax.axis_index("row")
    for bit in range(4):
        half = value.shape[0] // 2
        upper = place >> bit & 1
        kept = lax.dynamic_slice_in_dim(value, upper * half, half)
        sent = lax.dynamic_slice_in_dim(value, (1 - upper) * half, half)
        value = (kept.astype(F32) + partner(sent, "row", bit).astype(F32)).astype(BF16)
    for bit in reversed(range(4)):
        upper = place >> bit & 1 == 1
        theirs = partner(value, "row", bit)
        value = jnp.where(
            upper, jnp.concatenate([theirs, value], axis=0), jnp.concatenate([value, theirs], axis=0)
        )
    return value


def sum_small(value):
    for bit in range(4):
        value = value + partner(value, "row", bit)
    return value


def branch_tags(doc_ids, valid, place, unit):
    tags = jnp.where(valid == 1, doc_ids + 1, 0).reshape(16, 64, 2, 2, 2, 2)
    tags = tags.transpose(0, 5, 4, 3, 2, 1).reshape(16, SEG0)
    tags = jnp.take(tags, jnp.arange(16, dtype=jnp.int32) ^ place, axis=0)
    bit0, bit1, bit2 = place & 1, place >> 1 & 1, place >> 2 & 1
    dl = 4 * bit0 + 2 * bit1 + bit2
    result = [jnp.broadcast_to(tags[0][None, None], (8, 1, SEG0))]
    for branch in range(1, 5):
        rows = []
        size = SEG0 >> branch
        for relative in range(8 >> min(branch, 3)):
            group = (8 * unit + (relative ^ dl)) % 2**branch
            start = bitrev(group, branch) * size
            rows.append(lax.dynamic_slice(tags[: 2**branch], (0, start), (2**branch, size)).reshape(1, SEG0))
        result.append(jnp.stack(rows))
    return result, dl


def local(
    tokens,
    doc_ids,
    valid,
    ln1_gain,
    ln1_shift,
    w_query,
    b_query,
    w_key,
    w_value,
    b_value,
    w_out,
    b_out,
    ln2_gain,
    ln2_shift,
    w_up,
    b_up,
    w_down,
    b_down,
    cotangent,
):
    width = HEADS_HERE * HEAD_DIM
    scaling = HEAD_DIM**-0.5
    unit = lax.axis_index("unit")
    row = lax.axis_index("row")
    tags, dl = branch_tags(doc_ids, valid, row, unit)
    place = jnp.stack([dl, unit]).astype(jnp.int32)

    everything, sent, normed_t = project_call(
        place, tokens, ln1_gain, ln1_shift, w_query, b_query, w_key, w_value, b_value
    )
    parts = send_down(sent, True)
    out0, lse0 = forward_call(0, [everything], tags[0])
    outs = [forward_call(branch, parts, tags[branch])[0] for branch in range(1, 5)]
    back = send_up(*outs)
    merged_t, total = merge_call(place, out0, lse0, back)
    merged_low = merged_t.astype(BF16)

    order = one_hot_rows(True)
    residual = jnp.dot(order, tokens, preferred_element_type=F32)
    cot = jnp.dot(order, cotangent, preferred_element_type=F32).astype(BF16)

    def both_units(part):
        low = part.astype(BF16)
        return low.astype(F32) + swap_unit(low).astype(F32)

    attention = both_units(lax.dot_general(merged_low, w_out, TN, preferred_element_type=F32)) + b_out
    middle = residual + attention
    normed2 = layer_norm(middle, ln2_gain, ln2_shift)
    normed2_low = normed2.astype(BF16)
    up_input = jnp.dot(normed2_low, w_up, preferred_element_type=F32) + b_up
    hidden_low = gelu_tanh(up_input).astype(BF16)
    back_rows = cot.astype(F32)
    hidden_grad = lax.dot_general(cot, w_down, NT, preferred_element_type=F32)
    _, gelu_pull = jax.vjp(gelu_tanh, up_input)
    up_grad = gelu_pull(hidden_grad)[0].astype(BF16)
    normed2_grad = both_units(lax.dot_general(up_grad, w_up, NT, preferred_element_type=F32))
    feed_out = both_units(jnp.dot(hidden_low, w_down, preferred_element_type=F32)) + b_down
    mixed_out = (middle + feed_out).astype(BF16)
    grad_b_down = jnp.sum(back_rows, axis=0)
    grad_w_down = lax.dot_general(hidden_low, cot, TN, preferred_element_type=F32)
    grad_b_up = jnp.sum(up_grad.astype(F32), axis=0)
    grad_w_up = lax.dot_general(normed2_low, up_grad, TN, preferred_element_type=F32)
    _, norm2_pull = jax.vjp(layer_norm, middle, ln2_gain, ln2_shift)
    middle_part, grad_ln2_gain, grad_ln2_shift = norm2_pull(normed2_grad)
    middle_grad = back_rows + middle_part
    attention_grad = middle_grad.astype(BF16)
    grad_b_out = jnp.sum(attention_grad.astype(F32), axis=0)
    grad_w_out = jnp.dot(merged_low, attention_grad, preferred_element_type=F32)
    merged_grad = lax.dot_general(w_out, attention_grad, NT, preferred_element_type=F32).astype(BF16)

    grad_w_up, grad_w_down, grad_w_out = lax.psum(
        (grad_w_up.astype(BF16), grad_w_down.astype(BF16), grad_w_out.astype(BF16)), "row"
    )

    grads_all, grads_sent = spread_call(place, merged_grad, merged_t, total)
    grad_parts = send_down(grads_sent, False)
    own_grads = backward_call(0, [everything], [grads_all], tags[0])[0]
    back1, back2, back3 = [backward_call(b, parts, grad_parts, tags[b])[0] for b in (1, 2, 3)]
    back4, back4_kv = backward_call(4, parts, grad_parts, tags[4])
    other_kv = partner(back4_kv, "row", 3)
    back4 = jnp.concatenate(
        [back4[:, :HEAD_DIM], (back4[:, HEAD_DIM:].astype(F32) + other_kv.astype(F32)).astype(BF16)], axis=1
    )
    grads_back = send_up(back1, back2, back3, back4)
    qkv_grad = collect_call(place, own_grads, grads_back)
    query_grad, key_grad, value_grad = (qkv_grad[at * width : (at + 1) * width] for at in range(3))

    grad_w_qkv = lax.dot_general(normed_t, qkv_grad, NT, preferred_element_type=F32)
    grad_b_query = scaling * jnp.sum(query_grad.astype(F32), axis=1)
    grad_b_value = jnp.sum(value_grad.astype(F32), axis=1)
    normed_part = (
        scaling * lax.dot_general(query_grad, w_query, (((0,), (1,)), ((), ())), preferred_element_type=F32)
        + lax.dot_general(key_grad, w_key, (((0,), (1,)), ((), ())), preferred_element_type=F32)
        + lax.dot_general(value_grad, w_value, (((0,), (1,)), ((), ())), preferred_element_type=F32)
    )
    normed_grad = both_units(normed_part)
    _, norm1_pull = jax.vjp(layer_norm, residual, ln1_gain, ln1_shift)
    input_part, grad_ln1_gain, grad_ln1_shift = norm1_pull(normed_grad)
    grad_tokens = middle_grad + input_part

    summed_qkv = sum_rows(grad_w_qkv.astype(BF16)).astype(F32)
    grad_w_query, grad_w_key, grad_w_value = (summed_qkv[:, at * width : (at + 1) * width] for at in range(3))
    vectors = (
        grad_ln1_gain,
        grad_ln1_shift,
        grad_b_query,
        grad_b_value,
        grad_b_out,
        grad_ln2_gain,
        grad_ln2_shift,
        grad_b_up,
        grad_b_down,
    )
    lengths = [vector.shape[0] for vector in vectors]
    flat = sum_small(jnp.concatenate(vectors).reshape(-1, 128)).reshape(-1)
    ends = [sum(lengths[: at + 1]) for at in range(len(lengths))]
    (
        grad_ln1_gain,
        grad_ln1_shift,
        grad_b_query,
        grad_b_value,
        grad_b_out,
        grad_ln2_gain,
        grad_ln2_shift,
        grad_b_up,
        grad_b_down,
    ) = (flat[end - length : end] for end, length in zip(ends, lengths))

    disorder = one_hot_rows(False)
    mixed_out = jnp.dot(disorder, mixed_out, preferred_element_type=F32).astype(BF16)
    high = grad_tokens.astype(BF16)
    low = (grad_tokens - high.astype(F32)).astype(BF16)
    grad_tokens = jnp.dot(disorder, high, preferred_element_type=F32) + jnp.dot(
        disorder, low, preferred_element_type=F32
    )
    return (
        mixed_out,
        grad_tokens,
        grad_ln1_gain,
        grad_ln1_shift,
        grad_w_query * scaling,
        grad_b_query,
        grad_w_key,
        grad_w_value,
        grad_b_value,
        grad_w_out.astype(F32),
        grad_b_out,
        grad_ln2_gain,
        grad_ln2_shift,
        grad_w_up.astype(F32),
        grad_b_up,
        grad_w_down.astype(F32),
        grad_b_down,
    )


def solution(mesh):
    placed = (
        P("row", None),
        P(),
        P(),
        P(),
        P(),
        P(None, "unit"),
        P("unit"),
        P(None, "unit"),
        P(None, "unit"),
        P("unit"),
        P("unit", None),
        P(),
        P(),
        P(),
        P(None, "unit"),
        P("unit"),
        P("unit", None),
        P(),
        P("row", None),
    )
    rows = dict(mesh.shape)["row"]
    fast = rows == 16 and dict(mesh.shape)["unit"] == 2
    return jax.shard_map(
        local if fast else local_general,
        mesh=mesh,
        in_specs=placed,
        out_specs=(
            P("row", None),
            P("row", None),
            P(),
            P(),
            P(None, "unit"),
            P("unit"),
            P(None, "unit"),
            P(None, "unit"),
            P("unit"),
            P("unit", None),
            P(),
            P(),
            P(),
            P(None, "unit"),
            P("unit"),
            P("unit", None),
            P(),
        ),
        check_vma=False,
    )
```

```python
from functools import partial, reduce
import math

import jax
import jax.numpy as jnp
from jax import lax
from jax.experimental import pallas as pl
from jax.experimental.pallas import tpu as pltpu
from jax.sharding import PartitionSpec as P

HEAD_DIM = 48
SEG0 = 1024
BRANCHES = 5


EPSILON = 1e-05
MASKED = -1000000000.0
GELU_SCALE = 0.7978845608028654
F32 = jnp.float32
BF16 = jnp.bfloat16
HEADS_HERE = 8
QKV = 3 * HEAD_DIM
AUG = 16
OUT_ROWS = HEAD_DIM + AUG
NT = (((1,), (1,)), ((), ()))
TN = (((0,), (0,)), ((), ()))


def partner(value, axis, bit):
    mask = 2**bit
    pairs = [(source, source ^ mask) for source in range(lax.axis_size(axis))]
    return lax.ppermute(value, axis, pairs)


def layer_norm(values, norm_gain, norm_shift):
    row_mean = jnp.mean(values, axis=-1, keepdims=True)
    centred = values - row_mean
    row_var = jnp.mean(centred * centred, axis=-1, keepdims=True)
    return centred * lax.rsqrt(row_var + EPSILON) * norm_gain + norm_shift


def gelu_tanh(values):
    cubic = values + 0.044715 * values * values * values
    return 0.5 * values * (1.0 + jnp.tanh(GELU_SCALE * cubic))


def pick_rows(values, stride, offsets):
    count = offsets.shape[0]
    shaped = values.reshape((values.shape[0] // stride, stride) + values.shape[1:])
    chosen_mask = (jnp.arange(stride)[:, None] == offsets[None, :]).reshape(
        (1, stride, count) + (1,) * (values.ndim - 2)
    )
    chosen = jnp.sum(
        jnp.where(chosen_mask, shaped, jnp.zeros((), values.dtype)), axis=1, dtype=values.dtype
    )
    return jnp.moveaxis(chosen, 1, 0)


def spread_rows(values, stride, offsets):
    count = offsets.shape[0]
    moved = jnp.moveaxis(values, 0, 1)
    chosen_mask = (jnp.arange(stride)[:, None] == offsets[None, :]).reshape(
        (1, stride, count) + (1,) * (values.ndim - 2)
    )
    full_rows = jnp.where(chosen_mask, moved[:, None], jnp.zeros((), values.dtype))
    return full_rows.reshape((moved.shape[0] * stride,) + moved.shape[1:])


def blockwise(kernel, operands, unit_count, row_count):
    block_size = math.gcd(unit_count, max(1, 512 // row_count))
    split_parts = tuple(
        (item.reshape((unit_count // block_size, block_size) + item.shape[1:]) for item in operands)
    )
    results = lax.map(lambda group_parts: kernel(*group_parts), split_parts)
    return tuple((item.reshape((unit_count,) + item.shape[2:]) for item in results))


def masked_scores(queries, key_units, query_tags, key_tags):
    scores = jnp.einsum("uqd,ukd->uqk", queries, key_units, preferred_element_type=jnp.float32)
    return jnp.where(query_tags[:, :, None] == key_tags[:, None, :], scores, MASKED)


def attend_block(queries, key_units, value_units, query_tags, key_tags):
    scores = masked_scores(queries, key_units, query_tags, key_tags)
    row_peak = jnp.max(scores, axis=-1, keepdims=True)
    weights = jnp.exp(scores - row_peak)
    weight_sum = jnp.sum(weights, axis=-1, keepdims=True)
    attn_probs = (weights / weight_sum).astype(jnp.bfloat16)
    outputs = jnp.einsum(
        "uqk,ukd->uqd", attn_probs, value_units, preferred_element_type=jnp.float32
    )
    return (outputs, row_peak[..., 0] + jnp.log(weight_sum[..., 0]))


def both_grads_block(
    queries, key_units, value_units, query_tags, key_tags, log_total, out_grad, lse_grad
):
    attn_probs = jnp.exp(
        masked_scores(queries, key_units, query_tags, key_tags) - log_total[:, :, None]
    )
    prob_grad = jnp.einsum(
        "uqd,ukd->uqk", out_grad, value_units, preferred_element_type=jnp.float32
    )
    inner_sum = jnp.sum(attn_probs * prob_grad, axis=-1, keepdims=True)
    score_grad = (attn_probs * (prob_grad - inner_sum + lse_grad[:, :, None])).astype(jnp.bfloat16)
    query_grad = jnp.einsum(
        "uqk,ukd->uqd", score_grad, key_units, preferred_element_type=jnp.float32
    )
    key_grad = jnp.einsum("uqk,uqd->ukd", score_grad, queries, preferred_element_type=jnp.float32)
    value_grad = jnp.einsum(
        "uqk,uqd->ukd",
        attn_probs.astype(jnp.bfloat16),
        out_grad,
        preferred_element_type=jnp.float32,
    )
    return (query_grad, key_grad, value_grad)


def double_up(blocks, levels, row_pos, sender):
    blocks = list(blocks)
    for bit_level in range(max(levels)):
        active = [member for member in range(len(blocks)) if levels[member] > bit_level]
        lengths = [blocks[member].shape[2] for member in active]
        joined = jnp.concatenate([blocks[member] for member in active], axis=2)
        received = sender(joined, bit_level)
        upper_half = row_pos >> bit_level & 1 == 1
        offset_at = 0
        for member, length in zip(active, lengths):
            theirs = lax.slice_in_dim(received, offset_at, offset_at + length, axis=2)
            own_part = blocks[member]
            blocks[member] = jnp.where(
                upper_half,
                jnp.concatenate([theirs, own_part], axis=2),
                jnp.concatenate([own_part, theirs], axis=2),
            )
            offset_at += length
    return blocks


def halve_down(blocks, levels, row_pos, sender):
    blocks = list(blocks)
    for bit_level in reversed(range(max(levels))):
        active = [member for member in range(len(blocks)) if levels[member] > bit_level]
        upper_half = row_pos >> bit_level & 1 == 1
        kept_parts = []
        sent_parts = []
        for member in active:
            half_len = blocks[member].shape[2] // 2
            lower_part = blocks[member][:, :, :half_len]
            upper_part = blocks[member][:, :, half_len:]
            kept_parts.append(jnp.where(upper_half, upper_part, lower_part))
            sent_parts.append(jnp.where(upper_half, lower_part, upper_part))
        received = sender(jnp.concatenate(sent_parts, axis=2), bit_level)
        offset_at = 0
        for member, kept_part in zip(active, kept_parts):
            length = kept_part.shape[2]
            blocks[member] = kept_part + lax.slice_in_dim(
                received, offset_at, offset_at + length, axis=2
            )
            offset_at += length
    return blocks


def local_general(
    tokens,
    doc_ids,
    valid,
    ln1_gain,
    ln1_shift,
    w_query,
    b_query,
    w_key,
    w_value,
    b_value,
    w_out,
    b_out,
    ln2_gain,
    ln2_shift,
    w_up,
    b_up,
    w_down,
    b_down,
    cotangent,
):
    rows_here = tokens.shape[0]
    local_width = w_query.shape[1]
    heads_here = local_width // HEAD_DIM
    scaling = HEAD_DIM ** (-0.5)
    unit_pos = lax.axis_index("unit")
    row_pos = lax.axis_index("row")
    head_ids = unit_pos * heads_here + jnp.arange(heads_here, dtype=jnp.int32)
    all_tags = jnp.where(valid == 1, doc_ids, -1).reshape(-1)
    own_tags = lax.dynamic_slice_in_dim(all_tags, row_pos * rows_here, rows_here)
    residual = tokens.astype(jnp.float32)
    normed = layer_norm(residual, ln1_gain, ln1_shift)
    normed_low = normed.astype(jnp.bfloat16)
    head_shape = (rows_here, heads_here, HEAD_DIM)
    query_all = (
        ((jnp.dot(normed_low, w_query, preferred_element_type=jnp.float32) + b_query) * scaling)
        .astype(jnp.bfloat16)
        .reshape(head_shape)
    )
    key_all = (
        jnp.dot(normed_low, w_key, preferred_element_type=jnp.float32)
        .astype(jnp.bfloat16)
        .reshape(head_shape)
    )
    value_all = (
        (jnp.dot(normed_low, w_value, preferred_element_type=jnp.float32) + b_value)
        .astype(jnp.bfloat16)
        .reshape(head_shape)
    )
    branch_plans = []
    for branch in range(BRANCHES):
        stride = 2**branch
        extent = SEG0 * stride
        group_size = max(1, extent // rows_here)
        branch_plans.append(
            (
                stride,
                group_size,
                group_size.bit_length() - 1,
                max(1, rows_here // extent),
                head_ids % stride,
            )
        )
    levels = [branch_plan[2] for branch_plan in branch_plans]
    local_kv = [
        jnp.stack(
            [
                pick_rows(key_all, branch_plan[0], branch_plan[4]),
                pick_rows(value_all, branch_plan[0], branch_plan[4]),
            ]
        )
        for branch_plan in branch_plans
    ]

    def send_pairs(joined, bit_level):
        return partner(joined, "row", bit_level)

    gathered = double_up(local_kv, levels, row_pos, send_pairs)
    saved_parts = []
    branch_outs = []
    branch_lses = []
    selections = []
    for branch in range(BRANCHES):
        stride, group_size, branch_levels, segments, offsets = branch_plans[branch]
        unit_count = heads_here * segments
        per_unit = rows_here // stride // segments
        block_start = row_pos // group_size * (group_size * rows_here)
        block_tags = lax.dynamic_slice_in_dim(all_tags, block_start, group_size * rows_here)
        key_tags = pick_rows(
            jnp.broadcast_to(block_tags[:, None], (group_size * rows_here, heads_here)),
            stride,
            offsets,
        )
        query_tags = pick_rows(
            jnp.broadcast_to(own_tags[:, None], (rows_here, heads_here)), stride, offsets
        )
        queries = pick_rows(query_all, stride, offsets)
        key_units = gathered[branch][0]
        value_units = gathered[branch][1]
        outputs, log_total = blockwise(
            attend_block,
            (queries, key_units, value_units, query_tags, key_tags),
            unit_count,
            per_unit,
        )
        saved_parts.append((queries, key_units, value_units, query_tags, key_tags, log_total))
        branch_outs.append(spread_rows(outputs, stride, offsets))
        branch_lses.append(spread_rows(log_total, stride, offsets))
        selections.append(jnp.arange(rows_here)[:, None] % stride == offsets[None, :])
    peak_lse = reduce(
        jnp.maximum,
        [
            jnp.where(mask_here, lse_here, MASKED)
            for mask_here, lse_here in zip(selections, branch_lses)
        ],
    )
    weights = [
        jnp.where(mask_here, jnp.exp(jnp.where(mask_here, lse_here, peak_lse) - peak_lse), 0.0)
        for mask_here, lse_here in zip(selections, branch_lses)
    ]
    weight_sum = reduce(jnp.add, weights)
    shares = [weight_here / weight_sum for weight_here in weights]
    merged = reduce(
        jnp.add,
        [share_here[:, :, None] * out_here for share_here, out_here in zip(shares, branch_outs)],
    )
    merged_low = merged.reshape(rows_here, local_width).astype(jnp.bfloat16)
    attention = (
        lax.psum(jnp.dot(merged_low, w_out, preferred_element_type=jnp.float32), "unit") + b_out
    )
    middle = residual + attention
    normed2 = layer_norm(middle, ln2_gain, ln2_shift)
    normed2_low = normed2.astype(jnp.bfloat16)
    up_input = jnp.dot(normed2_low, w_up, preferred_element_type=jnp.float32) + b_up
    hidden_low = gelu_tanh(up_input).astype(jnp.bfloat16)
    feed_out = (
        lax.psum(jnp.dot(hidden_low, w_down, preferred_element_type=jnp.float32), "unit") + b_down
    )
    mixed_out = (middle + feed_out).astype(jnp.bfloat16)
    back_rows = cotangent.astype(jnp.float32)
    grad_b_down = jnp.sum(back_rows, axis=0)
    grad_w_down = jnp.einsum("tf,td->fd", hidden_low, cotangent, preferred_element_type=jnp.float32)
    hidden_grad = jnp.einsum("td,fd->tf", cotangent, w_down, preferred_element_type=jnp.float32)
    _, gelu_pull = jax.vjp(gelu_tanh, up_input)
    up_grad_low = gelu_pull(hidden_grad)[0].astype(jnp.bfloat16)
    grad_b_up = jnp.sum(up_grad_low.astype(jnp.float32), axis=0)
    grad_w_up = jnp.einsum(
        "tc,tf->cf", normed2_low, up_grad_low, preferred_element_type=jnp.float32
    )
    normed2_grad = lax.psum(
        jnp.einsum("tf,cf->tc", up_grad_low, w_up, preferred_element_type=jnp.float32), "unit"
    )
    _, norm2_pull = jax.vjp(layer_norm, middle, ln2_gain, ln2_shift)
    middle_part, grad_ln2_gain, grad_ln2_shift = norm2_pull(normed2_grad)
    middle_grad = back_rows + middle_part
    attention_grad = middle_grad.astype(jnp.bfloat16)
    grad_b_out = jnp.sum(attention_grad.astype(jnp.float32), axis=0)
    grad_w_out = jnp.einsum(
        "tc,td->cd", merged_low, attention_grad, preferred_element_type=jnp.float32
    )
    merged_grad = jnp.einsum(
        "td,cd->tc", attention_grad, w_out, preferred_element_type=jnp.float32
    ).reshape(head_shape)
    share_grads = [jnp.sum(merged_grad * out_here, axis=-1) for out_here in branch_outs]
    mean_grad = reduce(
        jnp.add, [share_here * grad_here for share_here, grad_here in zip(shares, share_grads)]
    )
    out_grad_units = []
    lse_grad_units = []
    for branch in range(BRANCHES):
        stride, group_size, branch_levels, segments, offsets = branch_plans[branch]
        unit_count = heads_here * segments
        per_unit = rows_here // stride // segments
        out_grad_rows = (shares[branch][:, :, None] * merged_grad).astype(jnp.bfloat16)
        lse_grad_rows = shares[branch] * (share_grads[branch] - mean_grad)
        out_grad_units.append(pick_rows(out_grad_rows, stride, offsets))
        lse_grad_units.append(pick_rows(lse_grad_rows, stride, offsets))
    query_grad = jnp.zeros(head_shape, jnp.float32)
    key_grad = jnp.zeros(head_shape, jnp.float32)
    value_grad = jnp.zeros(head_shape, jnp.float32)
    returned = []
    for branch in range(BRANCHES):
        stride, group_size, branch_levels, segments, offsets = branch_plans[branch]
        unit_count = heads_here * segments
        per_unit = rows_here // stride // segments
        queries, key_units, value_units, query_tags, key_tags, log_total = saved_parts[branch]
        grad_q, grad_k, grad_v = blockwise(
            both_grads_block,
            (
                queries,
                key_units,
                value_units,
                query_tags,
                key_tags,
                log_total,
                out_grad_units[branch],
                lse_grad_units[branch],
            ),
            unit_count,
            per_unit,
        )
        query_grad = query_grad + spread_rows(grad_q, stride, offsets)
        returned.append(jnp.stack([grad_k, grad_v]))

    def send_grads(joined, bit_level):
        return partner(joined, "row", bit_level)

    returned = halve_down(returned, levels, row_pos, send_grads)
    for branch in range(BRANCHES):
        stride, group_size, branch_levels, segments, offsets = branch_plans[branch]
        key_grad = key_grad + spread_rows(returned[branch][0], stride, offsets)
        value_grad = value_grad + spread_rows(returned[branch][1], stride, offsets)
    query_low = query_grad.reshape(rows_here, local_width).astype(jnp.bfloat16)
    key_low = key_grad.reshape(rows_here, local_width).astype(jnp.bfloat16)
    value_low = value_grad.reshape(rows_here, local_width).astype(jnp.bfloat16)
    grad_b_query = scaling * jnp.sum(query_low.astype(jnp.float32), axis=0)
    grad_w_query = scaling * jnp.einsum(
        "tc,tk->ck", normed_low, query_low, preferred_element_type=jnp.float32
    )
    grad_w_key = jnp.einsum("tc,tk->ck", normed_low, key_low, preferred_element_type=jnp.float32)
    grad_w_value = jnp.einsum(
        "tc,tk->ck", normed_low, value_low, preferred_element_type=jnp.float32
    )
    grad_b_value = jnp.sum(value_low.astype(jnp.float32), axis=0)
    normed_part = (
        scaling * jnp.einsum("tk,ck->tc", query_low, w_query, preferred_element_type=jnp.float32)
        + jnp.einsum("tk,ck->tc", key_low, w_key, preferred_element_type=jnp.float32)
        + jnp.einsum("tk,ck->tc", value_low, w_value, preferred_element_type=jnp.float32)
    )
    normed_grad = lax.psum(normed_part, "unit")
    _, norm1_pull = jax.vjp(layer_norm, residual, ln1_gain, ln1_shift)
    input_part, grad_ln1_gain, grad_ln1_shift = norm1_pull(normed_grad)
    grad_tokens = middle_grad + input_part
    (
        grad_ln1_gain,
        grad_ln1_shift,
        grad_w_query,
        grad_b_query,
        grad_w_key,
        grad_w_value,
        grad_b_value,
        grad_w_out,
        grad_b_out,
        grad_ln2_gain,
        grad_ln2_shift,
        grad_w_up,
        grad_b_up,
        grad_w_down,
        grad_b_down,
    ) = lax.psum(
        (
            grad_ln1_gain,
            grad_ln1_shift,
            grad_w_query,
            grad_b_query,
            grad_w_key,
            grad_w_value,
            grad_b_value,
            grad_w_out,
            grad_b_out,
            grad_ln2_gain,
            grad_ln2_shift,
            grad_w_up,
            grad_b_up,
            grad_w_down,
            grad_b_down,
        ),
        "row",
    )
    return (
        mixed_out,
        grad_tokens,
        grad_ln1_gain,
        grad_ln1_shift,
        grad_w_query,
        grad_b_query,
        grad_w_key,
        grad_w_value,
        grad_b_value,
        grad_w_out,
        grad_b_out,
        grad_ln2_gain,
        grad_ln2_shift,
        grad_w_up,
        grad_b_up,
        grad_w_down,
        grad_b_down,
    )


def bitrev(value, bits):
    return sum((value >> at & 1) << (bits - 1 - at) for at in range(bits))


def class_lanes(head, branch):
    size = SEG0 >> branch
    start = bitrev(head % 2**branch, branch) * size
    return slice(start, start + size)


LANES0 = {1: (0, 512), 2: (512, 256), 3: (768, 128), 4: (896, 64)}
LANES1 = {2: (0, 512), 3: (512, 256), 4: (768, 128)}
LANES2 = {3: (0, 512), 4: (512, 256)}


def one_hot_rows(forward):
    row = lax.broadcasted_iota(jnp.int32, (SEG0, SEG0), 0)
    col = lax.broadcasted_iota(jnp.int32, (SEG0, SEG0), 1)
    place, slot = (row, col) if forward else (col, row)
    group = place // 64
    rev = (group & 1) * 8 + (group >> 1 & 1) * 4 + (group >> 2 & 1) * 2 + (group >> 3 & 1)
    return jnp.where(rev + 16 * (place % 64) == slot, 1.0, 0.0).astype(BF16)


def split_three(value):
    high = value.astype(BF16).astype(F32)
    rest = value - high
    mid = rest.astype(BF16).astype(F32)
    return high, mid, rest - mid


def rows_iota(count, lanes):
    return lax.broadcasted_iota(jnp.int32, (count, lanes), 0)


def column(vector):
    return jnp.broadcast_to(vector[None, :], (8, vector.shape[0])).T[:, :1]


def project_kernel(
    pos_ref,
    tok_ref,
    doc_ref,
    valid_ref,
    gain_ref,
    shift_ref,
    wq_ref,
    bq_ref,
    wk_ref,
    wv_ref,
    bv_ref,
    all_ref,
    own_ref,
    away_ref,
    normed_ref,
    tags0_ref,
    tags1_ref,
    tags2_ref,
    tags3_ref,
    tags4_ref,
    place_ref,
):
    dl = pos_ref[0]
    unit = pos_ref[1]
    device = pos_ref[2]
    values = tok_ref[...].astype(F32)
    centred = values - jnp.mean(values, axis=-1, keepdims=True)
    row_var = jnp.mean(centred * centred, axis=-1, keepdims=True)
    scaled = centred * lax.rsqrt(row_var + EPSILON)
    normed = (scaled * gain_ref[...][None, :] + shift_ref[...][None, :]).astype(BF16)
    order = one_hot_rows(False)
    normed_t = lax.dot_general(normed, order, TN, preferred_element_type=F32).astype(BF16)
    normed_ref[...] = normed_t

    def project(w_ref):
        return lax.dot_general(w_ref[...], normed_t, TN, preferred_element_type=F32)

    query = ((project(wq_ref) + column(bq_ref[...])) * HEAD_DIM**-0.5).astype(BF16)
    key = project(wk_ref).astype(BF16)
    value = (project(wv_ref) + column(bv_ref[...])).astype(BF16)
    for head in range(HEADS_HERE):
        own = slice(head * HEAD_DIM, (head + 1) * HEAD_DIM)
        heres = [part[own] for part in (query, key, value)]
        for at, here in enumerate(heres):
            all_ref[head, at * HEAD_DIM : (at + 1) * HEAD_DIM, :] = here
        store_classes(head, unit, dl, heres, own_ref, away_ref)

    tags = jnp.where(valid_ref[...] == 1, doc_ref[...] + 1, 0)
    rows = jnp.concatenate([tags[:, at * SEG0 : (at + 1) * SEG0] for at in range(16)], axis=0)
    placed = jnp.dot(rows.astype(F32).astype(BF16), order, preferred_element_type=F32)
    place_ref[...] = placed.astype(jnp.int32)
    relative = [place_ref[pl.ds(at ^ device, 1), :] for at in range(16)]
    tags0_ref[...] = relative[0]
    for branch, ref in ((1, tags1_ref), (2, tags2_ref), (3, tags3_ref), (4, tags4_ref)):
        heads = 8 >> min(branch, 3)
        for head in range(HEADS_HERE):

            @pl.when((head ^ dl) < heads)
            def _():
                blocks = [row[:, class_lanes(head, min(branch, 3))] for row in relative[: 2**branch]]
                if branch == 4:
                    blocks = [jnp.where(unit == 0, block[:, :64], block[:, 64:]) for block in blocks]
                ref[head ^ dl] = jnp.concatenate(blocks, axis=1)


def store_classes(head, unit, dl, heres, own_ref, away_ref):
    at = head ^ dl

    def store(ref):
        start_row = 0
        for here in heres:
            rows = slice(start_row, start_row + here.shape[0])
            start_row += here.shape[0]
            for branch in (1, 2, 3):
                start, size = LANES0[branch]
                ref[at & 3, rows, start : start + size] = here[:, class_lanes(head, branch)]
            both = here[:, class_lanes(head, 3)]
            picked = jnp.where(unit == 0, both[:, :64].astype(F32), both[:, 64:].astype(F32))
            ref[at & 3, rows, 896:960] = picked.astype(BF16)

    @pl.when(at < 4)
    def _():
        store(own_ref)

    @pl.when(at >= 4)
    def _():
        store(away_ref)


def whole_spec(shape):
    return pl.BlockSpec(shape, lambda *_: (0,) * len(shape))


def whole_call(kernel, name, place, args, out_shape, scratch=(), flops=10**8, transcendentals=0):
    moved = sum(math.prod(a.shape) * a.dtype.itemsize for a in list(args) + list(out_shape))
    return pl.pallas_call(
        kernel,
        grid_spec=pltpu.PrefetchScalarGridSpec(
            num_scalar_prefetch=1,
            grid=(1,),
            in_specs=[whole_spec(a.shape) for a in args],
            out_specs=[whole_spec(o.shape) for o in out_shape],
            scratch_shapes=scratch,
        ),
        out_shape=out_shape,
        name=name,
        cost_estimate=pl.CostEstimate(flops=flops, bytes_accessed=moved, transcendentals=transcendentals),
    )(place, *args)


def project_call(place, *args):
    width = HEADS_HERE * HEAD_DIM
    model = args[0].shape[1]
    out_shape = [
        jax.ShapeDtypeStruct((HEADS_HERE, QKV, SEG0), BF16),
        jax.ShapeDtypeStruct((4, QKV, 960), BF16),
        jax.ShapeDtypeStruct((4, QKV, 960), BF16),
        jax.ShapeDtypeStruct((model, SEG0), BF16),
        jax.ShapeDtypeStruct((1, SEG0), jnp.int32),
    ] + [jax.ShapeDtypeStruct((8 >> min(branch, 3), 1, SEG0), jnp.int32) for branch in range(1, 5)]
    return whole_call(
        project_kernel,
        "project",
        place,
        args,
        out_shape,
        scratch=[pltpu.VMEM((16, SEG0), jnp.int32)],
        flops=2 * SEG0 * model * (3 * width + SEG0),
    )


def key_tail(tags):
    at = rows_iota(AUG, tags.shape[1])
    return jnp.where((at == tags) | (at > 12), 1.0, 0.0).astype(BF16)


def query_tail(tags):
    at = rows_iota(AUG, tags.shape[1])
    return jnp.where((at == tags) | (at > 12), 0.0, MASKED)


def gather_rows(pieces, rows):
    return jnp.concatenate([ref[0, rows[0] : rows[1], :size] for ref, size in pieces], axis=1)


def forward_kernel(*refs, sizes, tile, packed):
    count = len(sizes)
    piece_refs, (tag_ref,) = refs[:count], refs[count : count + 1]
    outs = refs[count + 1 :]
    shared = count if len(sizes) < 5 else count - 1
    q_pieces = [(piece_refs[i], sizes[i]) for i in range(shared)]
    kv_pieces = q_pieces
    query = gather_rows(q_pieces, (0, HEAD_DIM))
    key = gather_rows(kv_pieces, (HEAD_DIM, 2 * HEAD_DIM))
    value = gather_rows(kv_pieces, (2 * HEAD_DIM, QKV))
    if shared < count:
        last = piece_refs[-1]
        key = jnp.concatenate([key, last[0, :HEAD_DIM, :]], axis=1)
        value = jnp.concatenate([value, last[0, HEAD_DIM : 2 * HEAD_DIM, :]], axis=1)
    tags = tag_ref[...].reshape(1, SEG0)
    keys = key.shape[1]
    key_rows = jnp.concatenate([key, key_tail(tags)], axis=0).T
    ones = jnp.where(rows_iota(AUG, keys) == 0, 1.0, 0.0).astype(BF16)
    value_aug = jnp.concatenate([value, ones], axis=0)
    query_aug = jnp.concatenate([query, query_tail(tags[:, : query.shape[1]]).astype(BF16)], axis=0)
    for start in range(0, query.shape[1], tile):
        lanes = slice(start, start + tile)
        scores = jnp.dot(key_rows, query_aug[:, lanes], preferred_element_type=F32)
        peak = jnp.max(scores, axis=0, keepdims=True)
        weights = jnp.exp(scores - peak).astype(BF16)
        summed = jnp.dot(value_aug, weights, preferred_element_type=F32)
        total = summed[HEAD_DIM : HEAD_DIM + 1]
        outputs = summed[:HEAD_DIM] / total
        lse = peak + jnp.log(total)
        if packed:
            (o_ref,) = outs
            o_ref[0, :HEAD_DIM, lanes] = outputs.astype(BF16)
            high, mid, low = split_three(lse)
            at = rows_iota(AUG, tile)
            tail = jnp.where(at == 0, high, jnp.where(at == 1, mid, jnp.where(at == 2, low, 0.0)))
            o_ref[0, HEAD_DIM:, lanes] = tail.astype(BF16)
        else:
            o_ref, lse_ref = outs
            o_ref[0, :, lanes] = outputs
            lse_ref[0, :, lanes] = lse


def backward_kernel(*refs, sizes, grad_sizes, tile, out_type):
    count, grads = len(sizes), len(grad_sizes)
    piece_refs = refs[:count]
    grad_refs = refs[count : count + grads]
    tag_ref, out_ref = refs[count + grads : count + grads + 2]
    kv_out_ref = refs[-1]
    shared = count if count < 5 else count - 1
    pieces = [(piece_refs[i], sizes[i]) for i in range(shared)]
    query = gather_rows(pieces, (0, HEAD_DIM))
    key = gather_rows(pieces, (HEAD_DIM, 2 * HEAD_DIM))
    value = gather_rows(pieces, (2 * HEAD_DIM, QKV))
    if shared < count:
        last = piece_refs[-1]
        key = jnp.concatenate([key, last[0, :HEAD_DIM, :]], axis=1)
        value = jnp.concatenate([value, last[0, HEAD_DIM : 2 * HEAD_DIM, :]], axis=1)
    grad_pieces = [(grad_refs[i], grad_sizes[i]) for i in range(grads)]
    grad = gather_rows(grad_pieces, (0, HEAD_DIM))
    tail = gather_rows(grad_pieces, (HEAD_DIM, OUT_ROWS)).astype(F32)
    tags = tag_ref[...].reshape(1, SEG0)
    keys, queries = key.shape[1], query.shape[1]
    key_rows = jnp.concatenate([key, key_tail(tags)], axis=0).T
    ones = jnp.where(rows_iota(AUG, keys) < 3, 1.0, 0.0).astype(BF16)
    value_rows = jnp.concatenate([value, ones], axis=0).T
    at = rows_iota(AUG, queries)
    mask = query_tail(tags[:, :queries])
    query_aug = jnp.concatenate([query, jnp.where(at > 12, tail, mask).astype(BF16)], axis=0)
    grad_aug = jnp.concatenate([grad, jnp.where(at < 3, tail, 0.0).astype(BF16)], axis=0)
    key_grad = jnp.zeros((HEAD_DIM, keys), F32)
    value_grad = jnp.zeros((HEAD_DIM, keys), F32)
    for start in range(0, queries, tile):
        lanes = slice(start, start + tile)
        probs = jnp.exp(jnp.dot(key_rows, query_aug[:, lanes], preferred_element_type=F32))
        prob_grad = jnp.dot(value_rows, grad_aug[:, lanes], preferred_element_type=F32)
        score_grad = (probs * prob_grad).astype(BF16)
        probs_low = probs.astype(BF16)
        out_ref[0, :HEAD_DIM, lanes] = jnp.dot(key, score_grad, preferred_element_type=F32).astype(out_type)
        key_grad = key_grad + lax.dot_general(query[:, lanes], score_grad, NT, preferred_element_type=F32)
        value_grad = value_grad + lax.dot_general(grad[:, lanes], probs_low, NT, preferred_element_type=F32)
    if shared < count:
        half = keys // 2
        out_ref[0, HEAD_DIM : 2 * HEAD_DIM, :] = key_grad[:, :half].astype(out_type)
        out_ref[0, 2 * HEAD_DIM :, :] = value_grad[:, :half].astype(out_type)
        kv_out_ref[0, :HEAD_DIM, :] = key_grad[:, half:].astype(out_type)
        kv_out_ref[0, HEAD_DIM:, :] = value_grad[:, half:].astype(out_type)
    else:
        out_ref[0, HEAD_DIM : 2 * HEAD_DIM, :] = key_grad.astype(out_type)
        out_ref[0, 2 * HEAD_DIM :, :] = value_grad.astype(out_type)


def lane_spec(rows, start, size):
    block = max(size, 128)
    return pl.BlockSpec((1, rows, block), lambda head, at=start // block: (head, 0, at))


def tag_spec(branch):
    if branch == 0:
        return whole_spec((1, SEG0))
    return pl.BlockSpec((1, 1, SEG0), lambda head: (head, 0, 0))


def branch_pieces(branch, parts):
    if branch == 0:
        return [(parts[0], 0, SEG0)]
    pieces = [(parts[0],) + LANES0[branch], (parts[1],) + LANES0[branch]]
    if branch > 1:
        pieces.append((parts[2],) + LANES1[branch])
    if branch > 2:
        pieces.append((parts[3],) + LANES2[branch])
    return pieces


def forward_call(branch, parts, tags):
    pieces = branch_pieces(branch, parts)
    queries = sum(piece[2] for piece in pieces)
    if branch == 4:
        pieces.append((parts[4], 0, 512))
    heads = 8 >> min(branch, 3)
    packed = branch > 0
    if packed:
        out_shape = [jax.ShapeDtypeStruct((heads, OUT_ROWS, queries), BF16)]
        out_specs = [pl.BlockSpec((1, OUT_ROWS, queries), lambda head: (head, 0, 0))]
    else:
        out_shape = [
            jax.ShapeDtypeStruct((heads, HEAD_DIM, queries), F32),
            jax.ShapeDtypeStruct((heads, 1, queries), F32),
        ]
        out_specs = [
            pl.BlockSpec((1, HEAD_DIM, queries), lambda head: (head, 0, 0)),
            pl.BlockSpec((1, 1, queries), lambda head: (head, 0, 0)),
        ]
    return pl.pallas_call(
        partial(forward_kernel, sizes=tuple(piece[2] for piece in pieces), tile=512, packed=packed),
        grid=(heads,),
        in_specs=[lane_spec(array.shape[1], start, size) for array, start, size in pieces]
        + [tag_spec(branch)],
        out_specs=out_specs,
        out_shape=out_shape,
        name=f"attend{branch}",
        cost_estimate=pl.CostEstimate(
            flops=heads * queries * SEG0 * 2 * 512, bytes_accessed=heads * SEG0 * 512, transcendentals=heads * queries * SEG0
        ),
    )(*[piece[0] for piece in pieces], tags)


def backward_call(branch, parts, grad_parts, tags):
    pieces = branch_pieces(branch, parts)
    grad_pieces = branch_pieces(branch, grad_parts)
    queries = sum(piece[2] for piece in pieces)
    heads = 8 >> min(branch, 3)
    out_type = F32 if branch == 0 else BF16
    out_shape = [jax.ShapeDtypeStruct((heads, QKV, queries), out_type)]
    if branch == 4:
        pieces.append((parts[4], 0, 512))
        out_shape.append(jax.ShapeDtypeStruct((heads, 2 * HEAD_DIM, 512), out_type))
    return pl.pallas_call(
        partial(
            backward_kernel,
            sizes=tuple(piece[2] for piece in pieces),
            grad_sizes=tuple(piece[2] for piece in grad_pieces),
            tile=512,
            out_type=out_type,
        ),
        grid=(heads,),
        in_specs=[lane_spec(array.shape[1], start, size) for array, start, size in pieces + grad_pieces]
        + [tag_spec(branch)],
        out_specs=[pl.BlockSpec((1,) + out.shape[1:], lambda head: (head, 0, 0)) for out in out_shape],
        out_shape=out_shape,
        name=f"attend_back{branch}",
        cost_estimate=pl.CostEstimate(
            flops=heads * queries * SEG0 * 2 * 768, bytes_accessed=heads * SEG0 * 1024, transcendentals=heads * queries * SEG0
        ),
    )(*[piece[0] for piece in pieces + grad_pieces], tags)


def assemble(outs, third, second, first, full_ref):
    out1, out2, out3, out4 = outs
    full_ref[0:4, :, 0:512] = out1[:, :, 0:512]
    full_ref[0:2, :, 512:768] = out2[:, :, 0:256]
    full_ref[2:4, :, 512:768] = second[:, :, 0:256]
    full_ref[0:1, :, 768:896] = out3[:, :, 0:128]
    full_ref[1:2, :, 768:896] = third[:, :, 0:128]
    full_ref[2:4, :, 768:896] = second[:, :, 512:640]
    full_ref[0:1, :, 896:960] = out4[:, :, 0:64]
    full_ref[1:2, :, 896:960] = third[:, :, 512:576]
    full_ref[2:4, :, 896:960] = second[:, :, 768:832]
    full_ref[4:8, :, 0:960] = first[...]


def branch_blocks(head, unit, ref, rows, at):
    blocks = []
    for branch in (1, 2, 3):
        start, size = LANES0[branch]
        blocks.append((class_lanes(head, branch), ref[at, rows[0] : rows[1], start : start + size].astype(F32)))
    last = ref[at, rows[0] : rows[1], 896:960].astype(F32)
    twice = jnp.concatenate([last, last], axis=1)
    lane = lax.broadcasted_iota(jnp.int32, twice.shape, 1)
    blocks.append((class_lanes(head, 3), twice, (lane >= 64) == (unit == 1)))
    return blocks


def merge_kernel(
    pos_ref, o_ref, lse_ref, out1, out2, out3, out4, third, second, first, merged_ref, low_ref, total_ref, back_ref
):
    dl = pos_ref[0]
    unit = pos_ref[1]
    assemble((out1, out2, out3, out4), third, second, first, back_ref)
    for head in range(HEADS_HERE):
        at = head ^ dl
        tails = branch_blocks(head, unit, back_ref, (HEAD_DIM, OUT_ROWS), at)
        full = [lse_ref[head]]
        for block in tails:
            lanes = block[0]
            value = block[1][0:1] + block[1][1:2] + block[1][2:3]
            if len(block) == 3:
                value = jnp.where(block[2][0:1], value, MASKED)
            pad = []
            if lanes.start:
                pad.append(jnp.full((1, lanes.start), MASKED, F32))
            pad.append(value)
            if lanes.stop < SEG0:
                pad.append(jnp.full((1, SEG0 - lanes.stop), MASKED, F32))
            full.append(jnp.concatenate(pad, axis=1))
        peak = reduce(jnp.maximum, full)
        weights = [jnp.exp(value - peak) for value in full]
        summed = reduce(jnp.add, weights)
        total_ref[head] = peak + jnp.log(summed)
        shares = [weight / summed for weight in weights]
        rows = slice(head * HEAD_DIM, (head + 1) * HEAD_DIM)
        merged_ref[rows, :] = o_ref[head] * shares[0]
        outs = branch_blocks(head, unit, back_ref, (0, HEAD_DIM), at)
        for block, share in zip(outs, shares[1:]):
            merged_ref[rows, block[0]] += block[1] * share[:, block[0]]
        low_ref[rows, :] = merged_ref[rows, :].astype(BF16)


def merge_call(place, outputs, lse, backs):
    width = HEADS_HERE * HEAD_DIM
    out_shape = [
        jax.ShapeDtypeStruct((width, SEG0), F32),
        jax.ShapeDtypeStruct((width, SEG0), BF16),
        jax.ShapeDtypeStruct((HEADS_HERE, 1, SEG0), F32),
    ]
    scratch = [pltpu.VMEM((HEADS_HERE, OUT_ROWS, SEG0), BF16)]
    return whole_call(merge_kernel, "merge", place, (outputs, lse) + backs, out_shape, scratch)


def spread_kernel(pos_ref, grad_ref, merged_ref, total_ref, all_ref, own_ref, away_ref):
    dl = pos_ref[0]
    unit = pos_ref[1]
    at = rows_iota(AUG, SEG0)
    for head in range(HEADS_HERE):
        rows = slice(head * HEAD_DIM, (head + 1) * HEAD_DIM)
        grad = grad_ref[rows, :]
        delta = jnp.sum(grad.astype(F32) * merged_ref[rows, :], axis=0, keepdims=True)
        parts = split_three(-delta) + split_three(-total_ref[head])
        tail = jnp.zeros((AUG, SEG0), F32)
        for row, part in zip((0, 1, 2, 13, 14, 15), parts):
            tail = jnp.where(at == row, part, tail)
        heres = (grad, tail.astype(BF16))
        all_ref[head, :HEAD_DIM, :] = heres[0]
        all_ref[head, HEAD_DIM:, :] = heres[1]
        store_classes(head, unit, dl, heres, own_ref, away_ref)


def spread_call(place, grad, merged, total):
    out_shape = [jax.ShapeDtypeStruct((HEADS_HERE, OUT_ROWS, SEG0), BF16)] + [
        jax.ShapeDtypeStruct((4, OUT_ROWS, 960), BF16)
    ] * 2
    return whole_call(spread_kernel, "spread", place, (grad, merged, total), out_shape)


def collect_kernel(pos_ref, grad_ref, out1, out2, out3, out4, third, second, first, out_ref, sum_ref, back_ref):
    dl = pos_ref[0]
    unit = pos_ref[1]
    width = HEADS_HERE * HEAD_DIM
    assemble((out1, out2, out3, out4), third, second, first, back_ref)
    for head in range(HEADS_HERE):
        sum_ref[...] = grad_ref[head]
        for block in branch_blocks(head, unit, back_ref, (0, QKV), head ^ dl):
            value = block[1] if len(block) == 2 else jnp.where(block[2], block[1], 0.0)
            sum_ref[:, block[0]] += value
        for at in range(3):
            out_ref[at * width + head * HEAD_DIM : at * width + (head + 1) * HEAD_DIM, :] = sum_ref[
                at * HEAD_DIM : (at + 1) * HEAD_DIM, :
            ].astype(BF16)


def collect_call(place, own, backs):
    out_shape = [jax.ShapeDtypeStruct((HEADS_HERE * QKV, SEG0), BF16)]
    scratch = [pltpu.VMEM((QKV, SEG0), F32), pltpu.VMEM((HEADS_HERE, QKV, SEG0), BF16)]
    return whole_call(collect_kernel, "collect", place, (own,) + backs, out_shape, scratch)[0]


def swap_unit(value):
    return lax.ppermute(value, "unit", [(0, 1), (1, 0)])


def copy_kernel(*refs, moves):
    out_ref = refs[-1]
    for source, heads_from, rows, lanes_from, heads_to, lanes_to in moves:
        out_ref[heads_to, :, lanes_to] = refs[source][heads_from, rows, lanes_from]


def pack(name, arrays, moves, shape):
    def span(pair):
        return slice(pair[0], pair[0] + pair[1])

    moves = tuple((m[0], span(m[1]), span(m[2]), span(m[3]), span(m[4]), span(m[5])) for m in moves)
    out = jax.ShapeDtypeStruct(shape, BF16)
    return pl.pallas_call(
        partial(copy_kernel, moves=moves),
        out_shape=out,
        name=name,
        cost_estimate=pl.CostEstimate(flops=0, bytes_accessed=4 * math.prod(shape), transcendentals=0),
    )(*arrays)


def pack_down1(own, first):
    rows = (0, own.shape[1])
    moves = []
    at = 0
    for branch in (2, 3, 4):
        size = LANES0[branch][1]
        for source in (0, 1):
            moves.append((source, (2, 2), rows, LANES0[branch], (0, 2), (at, size)))
            at += size
    return pack("pack_down1", (own, first), moves, (2, rows[1], 896))


def pack_down2(own, first, second):
    rows = (0, own.shape[1])
    moves = []
    at = 0
    for branch in (3, 4):
        for source, lanes in ((0, LANES0[branch]), (1, LANES0[branch]), (2, LANES1[branch])):
            moves.append((source, (1, 1), rows, lanes, (0, 1), (at, lanes[1])))
            at += lanes[1]
    return pack("pack_down2", (own, first, second), moves, (1, rows[1], 768))


def pack_down3(own, first, second, third):
    rows = (HEAD_DIM, 2 * HEAD_DIM)
    moves = []
    at = 0
    for source, lanes in ((0, LANES0[4]), (1, LANES0[4]), (2, LANES1[4]), (3, LANES2[4])):
        moves.append((source, (0, 1), rows, lanes, (0, 1), (at, lanes[1])))
        at += lanes[1]
    return pack("pack_down3", (own, first, second, third), moves, (1, rows[1], 512))


def pack_up2(out3, out4):
    rows = (0, out3.shape[1])
    moves = [(0, (0, 1), rows, (512, 512), (0, 1), (0, 512)), (1, (0, 1), rows, (256, 256), (0, 1), (512, 256))]
    return pack("pack_up2", (out3, out4), moves, (1, rows[1], 768))


def pack_up1(out2, out3, out4, third):
    rows = (0, out3.shape[1])
    moves = [
        (0, (0, 2), rows, (512, 512), (0, 2), (0, 512)),
        (1, (0, 1), rows, (256, 256), (0, 1), (512, 256)),
        (3, (0, 1), rows, (256, 256), (1, 1), (512, 256)),
        (2, (0, 1), rows, (128, 128), (0, 1), (768, 128)),
        (3, (0, 1), rows, (640, 128), (1, 1), (768, 128)),
    ]
    return pack("pack_up1", (out2, out3, out4, third), moves, (2, rows[1], 896))


def pack_up0(out1, out2, out3, out4, third, second):
    rows = (0, out3.shape[1])
    moves = [
        (0, (0, 4), rows, (512, 512), (0, 4), (0, 512)),
        (1, (0, 2), rows, (256, 256), (0, 2), (512, 256)),
        (5, (0, 2), rows, (256, 256), (2, 2), (512, 256)),
        (2, (0, 1), rows, (128, 128), (0, 1), (768, 128)),
        (4, (0, 1), rows, (128, 128), (1, 1), (768, 128)),
        (5, (0, 2), rows, (640, 128), (2, 2), (768, 128)),
        (3, (0, 1), rows, (64, 64), (0, 1), (896, 64)),
        (4, (0, 1), rows, (576, 64), (1, 1), (896, 64)),
        (5, (0, 2), rows, (832, 64), (2, 2), (896, 64)),
    ]
    return pack("pack_up0", (out1, out2, out3, out4, third, second), moves, (4, rows[1], 960))


def after(value, *others):
    return lax.optimization_barrier((value,) + others)[0]


def sum_rows(value):
    place = lax.axis_index("row")
    for bit in range(4):
        half = value.shape[0] // 2
        upper = place >> bit & 1
        kept = lax.dynamic_slice_in_dim(value, upper * half, half)
        sent = lax.dynamic_slice_in_dim(value, (1 - upper) * half, half)
        value = (kept.astype(F32) + partner(sent, "row", bit).astype(F32)).astype(BF16)
    for bit in reversed(range(4)):
        upper = place >> bit & 1 == 1
        theirs = partner(value, "row", bit)
        value = jnp.where(
            upper, jnp.concatenate([theirs, value], axis=0), jnp.concatenate([value, theirs], axis=0)
        )
    return value


def sum_small(value):
    for bit in range(4):
        value = value + partner(value, "row", bit)
    return value


def local(
    tokens,
    doc_ids,
    valid,
    ln1_gain,
    ln1_shift,
    w_query,
    b_query,
    w_key,
    w_value,
    b_value,
    w_out,
    b_out,
    ln2_gain,
    ln2_shift,
    w_up,
    b_up,
    w_down,
    b_down,
    cotangent,
):
    width = HEADS_HERE * HEAD_DIM
    scaling = HEAD_DIM**-0.5
    unit = lax.axis_index("unit")
    row = lax.axis_index("row")
    dl = 4 * (row & 1) + 2 * (row >> 1 & 1) + (row >> 2 & 1)
    place = jnp.stack([dl, unit, row]).astype(jnp.int32)

    everything, own, away, normed_t, *tags = project_call(
        place, tokens, doc_ids, valid, ln1_gain, ln1_shift, w_query, b_query, w_key, w_value, b_value
    )
    first = partner(away, "row", 0)
    out0, lse0 = forward_call(0, [everything], tags[0])
    first = after(first, out0)
    second = partner(pack_down1(own, first), "row", 1)
    out1 = forward_call(1, [own, first], tags[1])[0]
    second = after(second, out1)
    third = partner(pack_down2(own, first, second), "row", 2)
    out2 = forward_call(2, [own, first, second], tags[2])[0]
    third = after(third, out2)
    fourth = partner(pack_down3(own, first, second, third), "row", 3)
    parts = [own, first, second, third, fourth]
    out3 = forward_call(3, parts, tags[3])[0]
    out4 = forward_call(4, parts, tags[4])[0]
    up_third = partner(pack_up2(out3, out4), "row", 2)
    up_second = partner(pack_up1(out2, out3, out4, up_third), "row", 1)
    up_first = partner(pack_up0(out1, out2, out3, out4, up_third, up_second), "row", 0)
    merged_t, merged_low, total = merge_call(
        place, out0, lse0, (out1, out2, out3, out4, up_third, up_second, up_first)
    )

    order = one_hot_rows(True)
    residual = jnp.dot(order, tokens, preferred_element_type=F32)
    cot = jnp.dot(order, cotangent, preferred_element_type=F32).astype(BF16)

    def both_units(part):
        low = part.astype(BF16)
        return low.astype(F32) + swap_unit(low).astype(F32)

    attention = both_units(lax.dot_general(merged_low, w_out, TN, preferred_element_type=F32)) + b_out
    middle = residual + attention
    normed2 = layer_norm(middle, ln2_gain, ln2_shift)
    normed2_low = normed2.astype(BF16)
    up_input = jnp.dot(normed2_low, w_up, preferred_element_type=F32) + b_up
    hidden_low = gelu_tanh(up_input).astype(BF16)
    back_rows = cot.astype(F32)
    hidden_grad = lax.dot_general(cot, w_down, NT, preferred_element_type=F32)
    _, gelu_pull = jax.vjp(gelu_tanh, up_input)
    up_grad = gelu_pull(hidden_grad)[0].astype(BF16)
    normed2_grad = both_units(lax.dot_general(up_grad, w_up, NT, preferred_element_type=F32))
    feed_out = both_units(jnp.dot(hidden_low, w_down, preferred_element_type=F32)) + b_down
    mixed_out = (middle + feed_out).astype(BF16)
    grad_b_down = jnp.sum(back_rows, axis=0)
    grad_w_down = lax.dot_general(hidden_low, cot, TN, preferred_element_type=F32)
    grad_b_up = jnp.sum(up_grad.astype(F32), axis=0)
    grad_w_up = lax.dot_general(normed2_low, up_grad, TN, preferred_element_type=F32)
    _, norm2_pull = jax.vjp(layer_norm, middle, ln2_gain, ln2_shift)
    middle_part, grad_ln2_gain, grad_ln2_shift = norm2_pull(normed2_grad)
    middle_grad = back_rows + middle_part
    attention_grad = middle_grad.astype(BF16)
    grad_b_out = jnp.sum(attention_grad.astype(F32), axis=0)
    grad_w_out = jnp.dot(merged_low, attention_grad, preferred_element_type=F32)
    merged_grad = lax.dot_general(w_out, attention_grad, NT, preferred_element_type=F32).astype(BF16)

    sums_in = (grad_w_up.astype(BF16), grad_w_down.astype(BF16), grad_w_out.astype(BF16))
    grad_w_up, grad_w_down, grad_w_out = lax.psum(sums_in, "row")

    merged_grad = after(merged_grad, *sums_in)
    grads_all, own_grad, away_grad = spread_call(place, merged_grad, merged_t, total)
    first_grad = partner(away_grad, "row", 0)
    main0 = backward_call(0, [everything], [grads_all], tags[0])[0]
    first_grad = after(first_grad, main0)
    second_grad = partner(pack_down1(own_grad, first_grad), "row", 1)
    back1 = backward_call(1, parts, [own_grad, first_grad], tags[1])[0]
    second_grad = after(second_grad, back1)
    third_grad = partner(pack_down2(own_grad, first_grad, second_grad), "row", 2)
    grad_parts = [own_grad, first_grad, second_grad, third_grad]
    back2 = backward_call(2, parts, grad_parts, tags[2])[0]
    grad_parts[3] = after(third_grad, back2)
    back4, back4_kv = backward_call(4, parts, grad_parts, tags[4])
    other_kv = partner(back4_kv, "row", 3)
    back3 = backward_call(3, parts, grad_parts, tags[3])[0]
    back4 = jnp.concatenate(
        [back4[:, :HEAD_DIM], (back4[:, HEAD_DIM:].astype(F32) + other_kv.astype(F32)).astype(BF16)], axis=1
    )
    up_third = partner(pack_up2(back3, back4), "row", 2)
    up_second = partner(pack_up1(back2, back3, back4, up_third), "row", 1)
    up_first = partner(pack_up0(back1, back2, back3, back4, up_third, up_second), "row", 0)
    qkv_grad = collect_call(place, main0, (back1, back2, back3, back4, up_third, up_second, up_first))
    query_grad, key_grad, value_grad = (qkv_grad[at * width : (at + 1) * width] for at in range(3))

    grad_w_qkv = lax.dot_general(normed_t, qkv_grad, NT, preferred_element_type=F32)
    grad_b_query = scaling * jnp.sum(query_grad.astype(F32), axis=1)
    grad_b_value = jnp.sum(value_grad.astype(F32), axis=1)
    normed_part = (
        scaling * lax.dot_general(query_grad, w_query, (((0,), (1,)), ((), ())), preferred_element_type=F32)
        + lax.dot_general(key_grad, w_key, (((0,), (1,)), ((), ())), preferred_element_type=F32)
        + lax.dot_general(value_grad, w_value, (((0,), (1,)), ((), ())), preferred_element_type=F32)
    )
    normed_grad = both_units(normed_part)
    _, norm1_pull = jax.vjp(layer_norm, residual, ln1_gain, ln1_shift)
    input_part, grad_ln1_gain, grad_ln1_shift = norm1_pull(normed_grad)
    grad_tokens = middle_grad + input_part

    summed_qkv = sum_rows(grad_w_qkv.astype(BF16)).astype(F32)
    grad_w_query, grad_w_key, grad_w_value = (summed_qkv[:, at * width : (at + 1) * width] for at in range(3))
    vectors = (
        grad_ln1_gain,
        grad_ln1_shift,
        grad_b_query,
        grad_b_value,
        grad_b_out,
        grad_ln2_gain,
        grad_ln2_shift,
        grad_b_up,
        grad_b_down,
    )
    lengths = [vector.shape[0] for vector in vectors]
    flat = sum_small(jnp.concatenate(vectors).reshape(-1, 128)).reshape(-1)
    ends = [sum(lengths[: at + 1]) for at in range(len(lengths))]
    (
        grad_ln1_gain,
        grad_ln1_shift,
        grad_b_query,
        grad_b_value,
        grad_b_out,
        grad_ln2_gain,
        grad_ln2_shift,
        grad_b_up,
        grad_b_down,
    ) = (flat[end - length : end] for end, length in zip(ends, lengths))

    disorder = one_hot_rows(False)
    mixed_out = jnp.dot(disorder, mixed_out, preferred_element_type=F32).astype(BF16)
    high = grad_tokens.astype(BF16)
    low = (grad_tokens - high.astype(F32)).astype(BF16)
    grad_tokens = jnp.dot(disorder, high, preferred_element_type=F32) + jnp.dot(
        disorder, low, preferred_element_type=F32
    )
    return (
        mixed_out,
        grad_tokens,
        grad_ln1_gain,
        grad_ln1_shift,
        grad_w_query * scaling,
        grad_b_query,
        grad_w_key,
        grad_w_value,
        grad_b_value,
        grad_w_out.astype(F32),
        grad_b_out,
        grad_ln2_gain,
        grad_ln2_shift,
        grad_w_up.astype(F32),
        grad_b_up,
        grad_w_down.astype(F32),
        grad_b_down,
    )


def solution(mesh):
    placed = (
        P("row", None),
        P(),
        P(),
        P(),
        P(),
        P(None, "unit"),
        P("unit"),
        P(None, "unit"),
        P(None, "unit"),
        P("unit"),
        P("unit", None),
        P(),
        P(),
        P(),
        P(None, "unit"),
        P("unit"),
        P("unit", None),
        P(),
        P("row", None),
    )
    rows = dict(mesh.shape)["row"]
    fast = rows == 16 and dict(mesh.shape)["unit"] == 2
    return jax.shard_map(
        local if fast else local_general,
        mesh=mesh,
        in_specs=placed,
        out_specs=(
            P("row", None),
            P("row", None),
            P(),
            P(),
            P(None, "unit"),
            P("unit"),
            P(None, "unit"),
            P(None, "unit"),
            P("unit"),
            P("unit", None),
            P(),
            P(),
            P(),
            P(None, "unit"),
            P("unit"),
            P("unit", None),
            P(),
        ),
        check_vma=False,
    )
```
